128 devices in a mesh: seq: 8 (over y, core), exp: 16 (over x, z).
Axes of the slice: x: 4, y: 4, z: 4, core: 2. Of those that a mesh axis runs over, the one named last changes fastest.
Arguments:
- moe_input: bfloat16 [1024, 4096], P('seq', 'exp'), may hold values from -6 to 6
- out_grad: bfloat16 [1024, 4096], P('seq', 'exp'), may hold values from -6 to 6
- expert_ids: int32 [1024, 2], P('seq'), may hold values from 0 to 7, all different within a row; in each aligned block of 128 rows (0 to 127, 128 to 255, ...) at most 48 rows name the same one
- expert_route_weights: float32 [1024, 2], P('seq'), may hold values from 0.1 to 1
- gate_weight: bfloat16 [16, 4096, 4096], P('exp', None, 'seq'), may hold values from -0.09375 to 0.09375
- up_weight: bfloat16 [16, 4096, 4096], P('exp', None, 'seq'), may hold values from -0.09375 to 0.09375
- down_weight: bfloat16 [16, 4096, 4096], P('exp', 'seq'), may hold values from -0.0625 to 0.0625
- out_weight: bfloat16 [8192, 4096], P(None, 'exp'), may hold values from -0.09375 to 0.09375
- scan_input: bfloat16 [8192, 1024], P('exp', 'seq'), may hold values from -6 to 6
- delta_raw: bfloat16 [8192, 1024], P('exp', 'seq'), may hold values from -1 to 1024
- mixer_gate_branch: bfloat16 [8192, 1024], P('exp', 'seq'), may hold values from -6 to 6
- state_input: float32 [16, 1024], P(None, 'seq'), may hold values from -0.25 to 0.25
- state_output: float32 [16, 1024], P(None, 'seq'), may hold values from -1.5 to 1.5
- log_rates: float32 [16, 8192], P(None, 'exp'), may hold values from -9 to -3
- skip_gain: float32 [8192], P('exp'), may hold values from 0.5 to 1.5
- block_states: float32 [8, 16, 8192], P('seq', None, 'exp'), may hold values from -6 to 6
Outputs:
- resid_grad: bfloat16 [1024, 4096], P('seq', 'exp')
- probs_grad: float32 [1024, 2], P('seq')
- input_grad: bfloat16 [8192, 1024], P('exp', 'seq')
- delta_grad: bfloat16 [8192, 1024], P('exp', 'seq')
- gate_grad: bfloat16 [8192, 1024], P('exp', 'seq')
- rates_grad: float32 [16, 8192], P(None, 'exp')
- skip_grad: float32 [8192], P('exp')
The draws below stay inside these ranges and needn't reach their ends.
Inputs may be any that keep to these rules, and one draw needn't show every extreme that they name: `expert_ids`: within each aligned block of 128 rows (one sequence shard) no expert is named by more than 48 rows, and in every draw some expert is named by exactly 48 rows of some block.
All inputs are finite; a program needn't handle non-finite values.
Results may differ from the reference program's by a relative error of at most 0.0052.
Values may be sent and summed in bfloat16 or wider, within the bound.
A program may use at most 128 MiB of HBM per device.

```python
import math
import jax
import jax.numpy as jnp
import numpy as np
from jax import lax

D = 4096
INNER = 8192
NSTATE = 16
TOP = 2
FFW = 8192
T_ROW = 128
EXPERTS = 8
CAP = 48
TOKEN_TOTAL = 1024
N_SEQ = 8


def packet_rows(key):
    chosen = jax.random.randint(jax.random.fold_in(key, 7), (2,), 0, TOKEN_TOTAL)
    places = jnp.arange(TOKEN_TOTAL)
    flagged = (places == chosen[0]) | (places == chosen[1])
    return flagged.astype(jnp.float32)


def draw_delta_raw(key, part):
    packet_groups = packet_rows(key)
    baseline_values = jax.random.uniform(jax.random.fold_in(key, 3), (INNER, TOKEN_TOTAL), jnp.float32, -0.5, 1.5)
    return (baseline_values * (1.0 - packet_groups[None, :]) + TOKEN_TOTAL * 1.0 * packet_groups[None, :]).astype(jnp.bfloat16)


def draw_state_input(key, part):
    packet_groups = packet_rows(key)
    baseline_values = 0.05 * jnp.clip(jax.random.normal(jax.random.fold_in(key, 11), (NSTATE, TOKEN_TOTAL), jnp.float32), -5.0, 5.0)
    return baseline_values * (1.0 - packet_groups[None, :]) + baseline_values * packet_groups[None, :] / (TOKEN_TOTAL * 1.0)


def draw_log_rates(key, part):
    levels = jax.random.uniform(jax.random.fold_in(key, 5), (NSTATE, INNER), jnp.float32)
    coin_flip = jax.random.uniform(jax.random.fold_in(key, 6), (NSTATE, INNER), jnp.float32)
    fast_share = 0.5
    fast_rate = math.log(1.0 / 50.0) + levels * math.log(50.0 / 30.0)
    slow_rate = jnp.log(0.25 / (TOKEN_TOTAL * 1.0)) + levels * math.log(0.6 / 0.25)
    slow_rate = jnp.maximum(slow_rate, -9.0)
    return jnp.where(coin_flip < fast_share, fast_rate, slow_rate)


def strengthened(array, stream_key, source, target, shards_of, factor):
    owner, partner = [(jnp.arange(array.shape[axis_at]) // (array.shape[axis_at] // shards_of)).reshape([-1 if axis == axis_at else 1 for axis in range(array.ndim)]) for axis_at in (source, target)]
    chosen = jax.random.permutation(stream_key, shards_of)[partner]
    strong = (owner == chosen) | (owner == (partner + shards_of // 2) % shards_of)
    return jnp.where(strong, factor * array, array)


def block_scale(key, dims, shards, smallest, largest):
    def one(axis_at, blocks):
        steps = jax.random.uniform(jax.random.fold_in(jax.random.fold_in(key, 6), axis_at), (blocks,), jnp.float32, smallest / len(shards), largest / len(shards))
        return jnp.repeat(jnp.exp(steps), dims[axis_at] // blocks).reshape((-1,) + (1,) * (len(dims) - axis_at - 1))

    gain = one(*shards[0])
    for cut in shards[1:]:
        gain = gain * one(*cut)
    return gain


def shared_out(key, own, number, rows, number_of, top, bound, skew):
    sequence = jax.random.permutation(key, number_of)
    heavy_load, ordinary = load_shares(number_of, rows * top, bound, skew, True), load_shares(number_of, rows * top, bound, skew, False)
    places = jnp.arange(number_of)

    def named(lengths, rotation):
        used = int((lengths > 0).sum())
        fixed = max(1, used // 4)
        moved = fixed + (places - fixed + rotation * (used - fixed)) % max(1, number_of - fixed)
        return jnp.zeros((number_of,), jnp.int32).at[sequence[jnp.where(places < fixed, places, moved)]].set(jnp.asarray(lengths, jnp.int32))

    lengths = jnp.where(number % 4 == 0, named(heavy_load, number // 4), named(ordinary, number - number // 4 - 1))
    mixed = jax.random.permutation(jax.random.fold_in(own, 3), number_of)
    giver, taker = mixed[0:number_of // 2 * 2:2], mixed[1:number_of // 2 * 2:2]
    margin = jnp.minimum(lengths[giver] - 1, bound - lengths[taker]) // 2
    margin = jnp.where((giver == sequence[0]) | (taker == sequence[0]) | (lengths[taker] == 0), 0, jnp.maximum(margin, 0))
    moved = jax.random.randint(jax.random.fold_in(own, 4), (number_of // 2,), 0, 1 << 20) % (margin + 1)
    lengths = lengths.at[giver].add(-moved).at[taker].add(moved)
    labels = jnp.searchsorted(jnp.cumsum(lengths), jnp.arange(rows * top), side="right").astype(jnp.int32)
    listing = labels.reshape(top, rows).T
    listing = listing[jax.random.permutation(jax.random.fold_in(own, 1), rows)]
    rotation = jax.random.randint(jax.random.fold_in(own, 2), (rows, 1), 0, top)
    return jnp.take_along_axis(listing, (jnp.arange(top)[None, :] + rotation) % top, axis=1)


def load_shares(count, total, most, slope, full):
    portions = [(1 << 20) // math.isqrt(standing ** slope) + 1 for standing in range(1, count + 1)]
    largest = most if full else min(most, max(-(-total // count), total * portions[0] // sum(portions)))
    least = 1 if total - largest >= count - 1 else 0
    holding, rest = [largest] + [least] * (count - 1), total - largest - least * (count - 1)
    while rest > 0:
        candidates = [i for i in range(1, count) if holding[i] < largest] or [i for i in range(1, count) if holding[i] < most]
        pool, left = sum([portions[i] for i in candidates]), rest
        for i in candidates:
            more = min(most - holding[i], max(1, left * portions[i] // pool), rest)
            holding[i] = holding[i] + more
            rest = rest - more
    return np.array(holding)


def centred(own_key, extent, spread, reach, cuts=(), held_as=jnp.bfloat16):
    array = spread * jax.random.normal(own_key, extent, jnp.float32)
    if cuts:
        array = array * block_scale(own_key, extent, cuts, -0.22, 0.18)
    return jnp.clip(array, -reach, reach).astype(held_as)


def noise_with(key, extent, width, reach, shards, heavy, kind=jnp.bfloat16):
    result = width * jax.random.normal(key, extent, jnp.float32)
    if shards:
        result = result * block_scale(key, extent, shards, -0.22, 0.18)
    return jnp.clip(strengthened(result, jax.random.fold_in(key, 3), *heavy), -reach, reach).astype(kind)


def setup_inputs(seed: int = 0) -> dict:
    streams_of = jax.random.split(jax.random.key(seed), 17)
    moe_input = centred(streams_of[0], (TOKEN_TOTAL, D), 1.0, 6.0, ((0, 8), (1, 16)))
    out_grad = centred(streams_of[1], (TOKEN_TOTAL, D), 1.0, 6.0, ((0, 8), (1, 16)))
    expert_ids_keys = jax.random.split(jax.random.fold_in(streams_of[2], 1), TOKEN_TOTAL // T_ROW)
    expert_ids_turns = jax.random.permutation(jax.random.fold_in(streams_of[2], 3), TOKEN_TOTAL // T_ROW)
    expert_ids = jax.vmap(lambda own, number: shared_out(jax.random.fold_in(streams_of[2], 2), own, number, T_ROW, EXPERTS, TOP, CAP, 2))(expert_ids_keys, expert_ids_turns).reshape((TOKEN_TOTAL, TOP))
    expert_route_weights = jnp.clip(0.1 + 0.9 * jax.random.uniform(streams_of[3], (TOKEN_TOTAL, TOP), jnp.float32) ** block_scale(streams_of[3], (TOKEN_TOTAL, TOP), ((0, 8),), -0.2, 0.2), 0.1, 1.0)
    gate_weight = centred(streams_of[4], (2 * EXPERTS, D, FFW // 2), D ** -0.5, 0.09375, ((0, 16), (2, 8)))
    up_weight = centred(streams_of[5], (2 * EXPERTS, D, FFW // 2), D ** -0.5, 0.09375, ((0, 16), (2, 8)))
    down_weight = centred(streams_of[6], (2 * EXPERTS, FFW // 2, D), FFW ** -0.5, 0.0625, ((0, 16), (1, 8)))
    out_weight = noise_with(streams_of[7], (INNER, D), INNER ** -0.5, 0.09375, ((1, 16),), (1, 0, 16, 2.0))
    scan_input = centred(streams_of[8], (INNER, TOKEN_TOTAL), 1.0, 6.0, ((0, 16), (1, 8)))
    delta_raw = draw_delta_raw(jax.random.fold_in(streams_of[16], 71), 0)
    mixer_gate_branch = centred(streams_of[10], (INNER, TOKEN_TOTAL), 1.0, 6.0, ((0, 16), (1, 8)))
    state_input = draw_state_input(jax.random.fold_in(streams_of[16], 71), 0)
    state_output = centred(streams_of[12], (NSTATE, TOKEN_TOTAL), 0.25, 1.5, ((1, 8),), jnp.float32)
    log_rates = draw_log_rates(jax.random.fold_in(streams_of[16], 71), 0)
    skip_gain = jnp.clip(0.5 + 1.0 * jax.random.uniform(streams_of[14], (INNER,), jnp.float32) ** block_scale(streams_of[14], (INNER,), ((0, 16),), -0.2, 0.2), 0.5, 1.5)
    block_states = centred(streams_of[15], (N_SEQ, NSTATE, INNER), 1.0, 6.0, ((0, 8), (2, 16)), jnp.float32)
    return dict(moe_input=moe_input, out_grad=out_grad, expert_ids=expert_ids, expert_route_weights=expert_route_weights, gate_weight=gate_weight, up_weight=up_weight, down_weight=down_weight, out_weight=out_weight, scan_input=scan_input, delta_raw=delta_raw, mixer_gate_branch=mixer_gate_branch, state_input=state_input, state_output=state_output, log_rates=log_rates, skip_gain=skip_gain, block_states=block_states)


def combine_maps(former, latter):
    return (former[0] * latter[0], latter[0] * former[1] + latter[1])


def affine_scan(decays, drives):
    return lax.associative_scan(combine_maps, (decays, drives), axis=decays.ndim - 1)


def reverse_scan(decays, drives):
    carried, summed = affine_scan(jnp.flip(decays, -1), jnp.flip(drives, -1))
    return jnp.flip(carried, -1), jnp.flip(summed, -1)


def reference(moe_input, out_grad, expert_ids, expert_route_weights, gate_weight, up_weight, down_weight, out_weight, scan_input, delta_raw, mixer_gate_branch, state_input, state_output, log_rates, skip_gain, block_states):
    slices = 2 * N_SEQ
    narrow = FFW // slices
    blocks = expert_ids.reshape(N_SEQ, T_ROW * TOP)
    matches = (blocks[:, :, None] == jnp.arange(EXPERTS, dtype=jnp.int32)[None, None, :]).astype(jnp.int32)
    slot_ids = jnp.sum((jnp.cumsum(matches, axis=1) - matches) * matches, axis=2)
    shard_idx = jnp.broadcast_to(jnp.arange(N_SEQ, dtype=jnp.int32)[:, None], blocks.shape)
    owners = shard_idx * T_ROW + jnp.arange(T_ROW * TOP, dtype=jnp.int32)[None, :] // TOP
    slot_table = jnp.zeros((EXPERTS, N_SEQ, CAP), jnp.int32).at[blocks, shard_idx, slot_ids].set(owners)
    contract = (((1,), (1,)), ((), ()))

    def expert_terms(inputs):
        chosen, gate_pair, up_pair, down_pair = inputs
        gate_full = jnp.concatenate([gate_pair[0], gate_pair[1]], axis=1)
        up_full = jnp.concatenate([up_pair[0], up_pair[1]], axis=1)
        down_full = jnp.concatenate([down_pair[0], down_pair[1]], axis=0)
        row_ids = chosen.reshape(N_SEQ * CAP)
        rows_in = moe_input[row_ids]
        rows_grad = out_grad[row_ids]
        gate_pre = jnp.dot(rows_in, gate_full, preferred_element_type=jnp.float32)
        up_pre = jnp.dot(rows_in, up_full, preferred_element_type=jnp.float32)
        hidden_grad = lax.dot_general(rows_grad, down_full, contract, preferred_element_type=jnp.float32)
        gate_sig = jax.nn.sigmoid(gate_pre)
        silu_gate = gate_pre * gate_sig
        row_count = N_SEQ * CAP
        probes = jnp.sum((silu_gate * up_pre * hidden_grad).reshape(row_count, slices, narrow), axis=2)
        probe_sum = jnp.sum(probes, axis=1)
        grad_up = (hidden_grad * silu_gate).astype(jnp.bfloat16)
        grad_gate = (hidden_grad * up_pre * gate_sig * (1.0 + gate_pre * (1.0 - gate_sig))).astype(jnp.bfloat16)
        split_gate = grad_gate.astype(jnp.float32).reshape(row_count, slices, narrow)
        split_up = grad_up.astype(jnp.float32).reshape(row_count, slices, narrow)
        gate_cols = gate_full.astype(jnp.float32).reshape(D, slices, narrow)
        up_cols = up_full.astype(jnp.float32).reshape(D, slices, narrow)
        slice_terms = jnp.einsum("mqh,dqh->qmd", split_gate, gate_cols, precision=lax.Precision.HIGHEST)
        slice_terms = slice_terms + jnp.einsum("mqh,dqh->qmd", split_up, up_cols, precision=lax.Precision.HIGHEST)
        route_sum = jnp.sum(slice_terms, axis=0)
        return route_sum.reshape(N_SEQ, CAP, D), probe_sum.reshape(N_SEQ, CAP)

    route_grads, probe_grads = lax.map(expert_terms, (slot_table, gate_weight.reshape(EXPERTS, 2, D, FFW // 2), up_weight.reshape(EXPERTS, 2, D, FFW // 2), down_weight.reshape(EXPERTS, 2, FFW // 2, D)))
    route_grad = route_grads[blocks, shard_idx, slot_ids].reshape(TOKEN_TOTAL, TOP, D)
    probs_grad = probe_grads[blocks, shard_idx, slot_ids].reshape(TOKEN_TOTAL, TOP)
    resid_grad = (out_grad.astype(jnp.float32) + jnp.sum(expert_route_weights[:, :, None] * route_grad, axis=1)).astype(jnp.bfloat16)
    inner_grad = jnp.dot(out_weight, resid_grad.T, preferred_element_type=jnp.float32)

    groups = 16
    group_width = INNER // groups

    def channel_group(inputs):
        u_raw, d_raw, z_raw, upstream, rates_log, skip_part, start_state = inputs
        signal = u_raw.astype(jnp.float32)
        time_step = jax.nn.softplus(d_raw.astype(jnp.float32))
        decay_rate = jnp.exp(rates_log)
        decays = jnp.exp(-time_step[None] * decay_rate[:, :, None])
        drives = time_step[None] * state_input[:, None, :] * signal[None]
        split_shape = (NSTATE, group_width, N_SEQ, T_ROW)
        carried, summed = affine_scan(decays.reshape(split_shape), drives.reshape(split_shape))
        entry = start_state[..., None]
        block_state = summed + carried * entry
        block_before = jnp.concatenate([entry, block_state[..., :-1]], axis=3)
        states = block_state.reshape(NSTATE, group_width, TOKEN_TOTAL)
        earlier = block_before.reshape(NSTATE, group_width, TOKEN_TOTAL)
        scan_out = jnp.sum(state_output[:, None, :] * states, axis=0) + skip_part[:, None] * signal
        gate_act = z_raw.astype(jnp.float32)
        gate_sig = jax.nn.sigmoid(gate_act)
        y_grad = upstream * gate_act * gate_sig
        gate_out = (upstream * scan_out * gate_sig * (1.0 + gate_act * (1.0 - gate_sig))).astype(jnp.bfloat16)
        shifted = jnp.concatenate([decays[:, :, 1:], jnp.ones((NSTATE, group_width, 1), jnp.float32)], axis=2)
        unused, adjoint = reverse_scan(shifted, state_output[:, None, :] * y_grad[None])
        input_out = (jnp.sum(adjoint * time_step[None] * state_input[:, None, :], axis=0) + skip_part[:, None] * y_grad).astype(jnp.bfloat16)
        step_grad = jnp.sum(adjoint * (state_input[:, None, :] * signal[None] - decay_rate[:, :, None] * decays * earlier), axis=0)
        delta_out = (step_grad * jax.nn.sigmoid(d_raw.astype(jnp.float32))).astype(jnp.bfloat16)
        rates_out = -decay_rate * jnp.sum(adjoint * time_step[None] * decays * earlier, axis=2)
        skip_out = jnp.sum(y_grad * signal, axis=1)
        return input_out, delta_out, gate_out, rates_out, skip_out

    group_inputs = (scan_input.reshape(groups, group_width, TOKEN_TOTAL), delta_raw.reshape(groups, group_width, TOKEN_TOTAL), mixer_gate_branch.reshape(groups, group_width, TOKEN_TOTAL), inner_grad.reshape(groups, group_width, TOKEN_TOTAL), jnp.transpose(log_rates.reshape(NSTATE, groups, group_width), (1, 0, 2)), skip_gain.reshape(groups, group_width), jnp.transpose(block_states.reshape(N_SEQ, NSTATE, groups, group_width), (2, 1, 3, 0)))
    input_grad, delta_grad, gate_grad, rates_grad, skip_grad = lax.map(channel_group, group_inputs)
    input_grad = input_grad.reshape(INNER, TOKEN_TOTAL)
    delta_grad = delta_grad.reshape(INNER, TOKEN_TOTAL)
    gate_grad = gate_grad.reshape(INNER, TOKEN_TOTAL)
    rates_grad = jnp.transpose(rates_grad, (1, 0, 2)).reshape(NSTATE, INNER)
    skip_grad = skip_grad.reshape(INNER)
    return (resid_grad, probs_grad, input_grad, delta_grad, gate_grad, rates_grad, skip_grad)
```

```python
import jax
import jax.numpy as jnp
from jax import lax
from jax.experimental import pallas as pl
from jax.experimental.pallas import tpu as pltpu
from jax.sharding import PartitionSpec as P

N_SEQ = 8
F32 = jnp.float32
BF16 = jnp.bfloat16
VMEM = pl.BlockSpec(memory_space=pltpu.VMEM)
SMEM = pl.BlockSpec(memory_space=pltpu.SMEM)


def shape(dims, kind=jnp.float32):
    return jax.ShapeDtypeStruct(dims, kind)


LOG2E = 1.4426950408889634
GR = 4
TT = 128


def softplus(v):
    return jnp.maximum(v, 0.0) + jnp.log1p(jnp.exp(-jnp.abs(v)))


def sigmoid(v):
    return 1.0 / (1.0 + jnp.exp(-v))


def spread(ref, g, val):
    ref[pl.ds(g, TT, stride=8), :] = val
    ref[pl.ds(GR + g, TT, stride=8), :] = val


def column(rep, t):
    return jnp.take_along_axis(rep, jnp.full((8, 128), t, jnp.int32), axis=1)


def forward_kernel(u_ref, d_ref, b_ref, c_ref, lr_ref, st_ref, sk_ref, ear_ref, dt_ref, us_ref, so_ref):
    for g in range(GR):
        rows = pl.ds(g * 128, 128)
        spread(dt_ref, g, softplus(d_ref[rows, :].astype(jnp.float32).T))
        spread(us_ref, g, u_ref[rows, :].astype(jnp.float32).T)
    rate2 = [-LOG2E * jnp.exp(lr_ref[8 * j:8 * j + 8, :]) for j in range(8)]
    skip = sk_ref[...]

    def step(t, states):
        here = pl.ds(pl.multiple_of(t * 8, 8), 8)
        dt = dt_ref[here, :]
        u = us_ref[here, :]
        du = dt * u
        acc = jnp.zeros((8, 128), jnp.float32)
        out = []
        for j in range(8):
            ear_ref[pl.ds(pl.multiple_of(t * 64, 64) + 8 * j, 8), :] = states[j]
            b = column(b_ref[8 * j:8 * j + 8, :], t)
            c = column(c_ref[8 * j:8 * j + 8, :], t)
            state = jnp.exp2(dt * rate2[j]) * states[j] + du * b
            acc = acc + c * state
            out.append(state)
        so_ref[here, :] = acc + pltpu.roll(acc, 4, 0) + skip * u
        return tuple(out)

    lax.fori_loop(0, TT, step, tuple(st_ref[8 * j:8 * j + 8, :] for j in range(8)), unroll=2)


def middle_kernel(in_ref, z_ref, c_ref, lr_ref, dt_ref, so_ref, y_ref, gate_ref, pair_ref):
    for g in range(GR):
        rows = pl.ds(g * 128, 128)
        up = in_ref[rows, :]
        z = z_ref[rows, :].astype(jnp.float32)
        sig = sigmoid(z)
        spread(y_ref, g, (up * z * sig).T)
        so = so_ref[pl.ds(g, TT, stride=8), :].T
        gate_ref[rows, :] = (up * so * sig * (1.0 + z * (1.0 - sig))).astype(jnp.bfloat16)
    rate2 = [-LOG2E * jnp.exp(lr_ref[8 * j:8 * j + 8, :]) for j in range(8)]

    def step(i, carry):
        t = TT - 1 - i
        here = pl.ds(pl.multiple_of(t * 8, 8), 8)
        dt = dt_ref[here, :]
        y = y_ref[here, :]
        total = carry[8] + dt
        out = []
        for j in range(8):
            c = column(c_ref[8 * j:8 * j + 8, :], t)
            out.append(jnp.exp2(dt * rate2[j]) * (c * y + carry[j]))
        return tuple(out) + (total,)

    zero = jnp.zeros((8, 128), jnp.float32)
    last = lax.fori_loop(0, TT, step, (zero,) * 9, unroll=2)
    for j in range(8):
        pair_ref[8 * j:8 * j + 8, :] = last[j]
        pair_ref[64 + 8 * j:72 + 8 * j, :] = jnp.exp2(rate2[j] * last[8])


def final_kernel(me_ref, all_ref, y_ref, ear_ref, dt_ref, us_ref, d_ref, b_ref, c_ref, lr_ref, sk_ref,
                 input_ref, delta_ref, part_ref, s1_ref, dl_ref):
    me = me_ref[0]
    rate = [jnp.exp(lr_ref[8 * j:8 * j + 8, :]) for j in range(8)]
    rate2 = [-LOG2E * rate[j] for j in range(8)]
    start = []
    for j in range(8):
        inc = jnp.zeros((8, 128), jnp.float32)
        for r in range(N_SEQ - 1, 0, -1):
            term = all_ref[r, 8 * j:8 * j + 8, :]
            decay = all_ref[r, 64 + 8 * j:72 + 8 * j, :]
            inc = jnp.where(r > me, term + decay * inc, inc)
        start.append(inc)

    def step(i, carry):
        vs, sums, sk = carry
        t = TT - 1 - i
        here = pl.ds(pl.multiple_of(t * 8, 8), 8)
        dt = dt_ref[here, :]
        y = y_ref[here, :]
        s1 = jnp.zeros((8, 128), jnp.float32)
        dl = jnp.zeros((8, 128), jnp.float32)
        nv, ns = [], []
        for j in range(8):
            b = column(b_ref[8 * j:8 * j + 8, :], t)
            c = column(c_ref[8 * j:8 * j + 8, :], t)
            adj = c * y + vs[j]
            v = jnp.exp2(dt * rate2[j]) * adj
            x = v * ear_ref[pl.ds(pl.multiple_of(t * 64, 64) + 8 * j, 8), :]
            s1 = s1 + adj * b
            dl = dl + rate[j] * x
            ns.append(sums[j] + dt * x)
            nv.append(v)
        s1_ref[here, :] = s1 + pltpu.roll(s1, 4, 0)
        dl_ref[here, :] = dl + pltpu.roll(dl, 4, 0)
        return tuple(nv), tuple(ns), sk + y * us_ref[here, :]

    zero = jnp.zeros((8, 128), jnp.float32)
    vs, sums, sk = lax.fori_loop(0, TT, step, (tuple(start), (zero,) * 8, zero), unroll=2)
    for j in range(8):
        part_ref[8 * j:8 * j + 8, :] = -rate[j] * sums[j]
    part_ref[64:72, :] = sk
    for g in range(GR):
        rows = pl.ds(g * 128, 128)
        mine = pl.ds(g, TT, stride=8)
        s1 = s1_ref[mine, :]
        inp = s1 * dt_ref[mine, :] + sk_ref[g:g + 1, :] * y_ref[mine, :]
        input_ref[rows, :] = inp.T.astype(jnp.bfloat16)
        step_grad = us_ref[mine, :] * s1 - dl_ref[mine, :]
        delta_ref[rows, :] = (step_grad.T * sigmoid(d_ref[rows, :].astype(jnp.float32))).astype(jnp.bfloat16)


def expert_backward(rows_in, rows_grad, gate_slice, up_slice, down_slice):
    contract = (((1,), (1,)), ((), ()))
    gate_pre = jnp.dot(rows_in, gate_slice, preferred_element_type=jnp.float32)
    up_pre = jnp.dot(rows_in, up_slice, preferred_element_type=jnp.float32)
    hidden_grad = lax.dot_general(
        rows_grad, down_slice, contract, preferred_element_type=jnp.float32
    )
    gate_sig = jax.nn.sigmoid(gate_pre)
    silu_gate = gate_pre * gate_sig
    probes = jnp.sum(silu_gate * up_pre * hidden_grad, axis=1)
    grad_up = (hidden_grad * silu_gate).astype(jnp.bfloat16)
    grad_gate = (hidden_grad * up_pre * gate_sig * (1.0 + gate_pre * (1.0 - gate_sig))).astype(
        jnp.bfloat16
    )
    partial_rows = lax.dot_general(
        grad_gate, gate_slice, contract, preferred_element_type=jnp.float32
    )
    partial_rows = partial_rows + lax.dot_general(
        grad_up, up_slice, contract, preferred_element_type=jnp.float32
    )
    return (partial_rows, probes)


def local(
    moe_input,
    out_grad,
    expert_ids,
    expert_route_weights,
    gate_weight,
    up_weight,
    down_weight,
    out_weight,
    scan_input,
    delta_raw,
    mixer_gate_branch,
    state_input,
    state_output,
    log_rates,
    skip_gain,
    block_states,
):
    seq_count = lax.axis_size("seq")
    exp_count = lax.axis_size("exp")
    row_count, feat_cols = moe_input.shape
    top_count = expert_ids.shape[1]
    experts = exp_count // 2
    capacity = 3 * top_count * row_count // (2 * experts)
    b_rep = jnp.repeat(state_input, GR, axis=0)
    c_rep = jnp.repeat(state_output, GR, axis=0)
    rates = log_rates.reshape(64, 128)
    start = block_states.reshape(64, 128)
    skip = jnp.tile(skip_gain.reshape(GR, 128), (2, 1))
    earlier, steps, signal, scan_out = pl.pallas_call(
        forward_kernel,
        out_shape=(shape((TT * 64, 128)), shape((TT * 8, 128)), shape((TT * 8, 128)), shape((TT * 8, 128))),
        in_specs=[VMEM] * 7,
        out_specs=(VMEM,) * 4,
        name="scan_forward",
    )(scan_input, delta_raw, b_rep, c_rep, rates, start, skip)
    flat_ids = expert_ids.reshape(row_count * top_count)
    matches = (flat_ids[:, None] == jnp.arange(experts, dtype=jnp.int32)[None, :]).astype(jnp.int32)
    slot_ids = jnp.sum((jnp.cumsum(matches, axis=0) - matches) * matches, axis=1)
    owners = jnp.arange(row_count * top_count, dtype=jnp.int32) // top_count
    slot_table = jnp.zeros((capacity, experts), jnp.int32).at[slot_ids, flat_ids].set(owners)
    send_in = moe_input[slot_table]
    send_grad = out_grad[slot_table]

    def widen_all(block):
        wide = jnp.broadcast_to(
            block[:, None, :, None, :], (capacity, seq_count, experts, 2, feat_cols)
        )
        return wide.reshape(capacity, seq_count * exp_count, feat_cols)

    got_in, got_grad = (
        lax.all_to_all(widen_all(send_in), ("seq", "exp"), split_axis=1, concat_axis=1, tiled=True),
        lax.all_to_all(
            widen_all(send_grad), ("seq", "exp"), split_axis=1, concat_axis=1, tiled=True
        ),
    )
    rows_in = got_in.reshape(capacity * seq_count, exp_count * feat_cols)
    rows_grad = got_grad.reshape(capacity * seq_count, exp_count * feat_cols)
    partial_rows, probes = expert_backward(
        rows_in, rows_grad, gate_weight[0], up_weight[0], down_weight[0]
    )
    part_back = partial_rows.reshape(capacity, seq_count * exp_count, feat_cols)
    probe_back = jnp.broadcast_to(
        probes.reshape(capacity, seq_count, 1, 1), (capacity, seq_count, exp_count, 1)
    ).reshape(capacity, seq_count * exp_count, 1)
    back_part, back_probe = (
        lax.all_to_all(part_back, ("seq", "exp"), split_axis=1, concat_axis=1, tiled=True),
        lax.all_to_all(probe_back, ("seq", "exp"), split_axis=1, concat_axis=1, tiled=True),
    )
    route_sum = jnp.sum(back_part.reshape(capacity, seq_count, experts, 2, feat_cols), axis=(1, 3))
    probe_sum = jnp.sum(back_probe.reshape(capacity, seq_count, experts, 2), axis=(1, 3))
    route_grad = route_sum[slot_ids, flat_ids].reshape(row_count, top_count, feat_cols)
    probs_grad = probe_sum[slot_ids, flat_ids].reshape(row_count, top_count)
    mixture = jnp.sum(expert_route_weights[:, :, None] * route_grad, axis=1)
    resid_grad = (out_grad.astype(jnp.float32) + mixture).astype(jnp.bfloat16)
    block = out_weight
    inner_grad = lax.psum_scatter(
        lax.dot_general(
            block, resid_grad, (((1,), (1,)), ((), ())), preferred_element_type=jnp.float32
        ),
        "exp",
        scatter_dimension=0,
        tiled=True,
    )
    y_grad, gate_grad, pair = pl.pallas_call(
        middle_kernel,
        out_shape=(shape((TT * 8, 128)), shape((512, 128), BF16), shape((128, 128))),
        in_specs=[VMEM] * 6,
        out_specs=(VMEM,) * 3,
        name="adjoint_summary",
    )(inner_grad, mixer_gate_branch, c_rep, rates, steps, scan_out)
    pairs = lax.all_gather(pair, "seq")
    me = lax.axis_index("seq").astype(jnp.int32).reshape(1)
    input_grad, delta_grad, part = pl.pallas_call(
        final_kernel,
        out_shape=(shape((512, 128), BF16), shape((512, 128), BF16), shape((72, 128))),
        in_specs=[SMEM] + [VMEM] * 10,
        out_specs=(VMEM,) * 3,
        scratch_shapes=[pltpu.VMEM((TT * 8, 128), F32)] * 2,
        name="adjoint_final",
    )(me, pairs, y_grad, earlier, steps, signal, delta_raw, b_rep, c_rep, rates, skip)
    total = lax.psum(part, "seq")
    rates_grad = total[:64].reshape(16, 512)
    skip_grad = total[64:68].reshape(512)
    return (resid_grad, probs_grad, input_grad, delta_grad, gate_grad, rates_grad, skip_grad)


def solution(mesh):
    in_specs = (
        P("seq", "exp"),
        P("seq", "exp"),
        P("seq", None),
        P("seq", None),
        P("exp", None, "seq"),
        P("exp", None, "seq"),
        P("exp", "seq", None),
        P(None, "exp"),
        P("exp", "seq"),
        P("exp", "seq"),
        P("exp", "seq"),
        P(None, "seq"),
        P(None, "seq"),
        P(None, "exp"),
        P("exp"),
        P("seq", None, "exp"),
    )
    out_specs = (
        P("seq", "exp"),
        P("seq", None),
        P("exp", "seq"),
        P("exp", "seq"),
        P("exp", "seq"),
        P(None, "exp"),
        P("exp"),
    )
    return jax.shard_map(local, mesh=mesh, in_specs=in_specs, out_specs=out_specs, check_vma=False)
```

```python
import jax
import jax.numpy as jnp
from jax import lax
from jax.experimental import pallas as pl
from jax.experimental.pallas import tpu as pltpu
from jax.sharding import PartitionSpec as P

N_SEQ = 8
F32 = jnp.float32
BF16 = jnp.bfloat16
VMEM = pl.BlockSpec(memory_space=pltpu.VMEM)
SMEM = pl.BlockSpec(memory_space=pltpu.SMEM)


def shape(dims, kind=jnp.float32):
    return jax.ShapeDtypeStruct(dims, kind)


LOG2E = 1.4426950408889634
GR = 4
TT = 128


def softplus(v):
    return jnp.maximum(v, 0.0) + jnp.log1p(jnp.exp(-jnp.abs(v)))


def sigmoid(v):
    return 1.0 / (1.0 + jnp.exp(-v))


def spread(ref, g, val):
    ref[pl.ds(g, TT, stride=8), :] = val
    ref[pl.ds(GR + g, TT, stride=8), :] = val


def column(rep, t):
    return jnp.take_along_axis(rep, jnp.full((8, 128), t, jnp.int32), axis=1)


def forward_kernel(u_ref, d_ref, b_ref, c_ref, lr_ref, st_ref, sk_ref, ear_ref, dt_ref, us_ref, so_ref):
    for g in range(GR):
        rows = pl.ds(g * 128, 128)
        spread(dt_ref, g, softplus(d_ref[rows, :].astype(jnp.float32).T))
        spread(us_ref, g, u_ref[rows, :].astype(jnp.float32).T)
    rate2 = [-LOG2E * jnp.exp(lr_ref[8 * j:8 * j + 8, :]) for j in range(8)]
    skip = sk_ref[...]

    def step(t, states):
        here = pl.ds(pl.multiple_of(t * 8, 8), 8)
        dt = dt_ref[here, :]
        u = us_ref[here, :]
        du = dt * u
        acc = jnp.zeros((8, 128), jnp.float32)
        out = []
        for j in range(8):
            ear_ref[pl.ds(pl.multiple_of(t * 64, 64) + 8 * j, 8), :] = states[j]
            b = column(b_ref[8 * j:8 * j + 8, :], t)
            c = column(c_ref[8 * j:8 * j + 8, :], t)
            state = jnp.exp2(dt * rate2[j]) * states[j] + du * b
            acc = acc + c * state
            out.append(state)
        so_ref[here, :] = acc + pltpu.roll(acc, 4, 0) + skip * u
        return tuple(out)

    lax.fori_loop(0, TT, step, tuple(st_ref[8 * j:8 * j + 8, :] for j in range(8)), unroll=2)


def middle_kernel(in_ref, z_ref, c_ref, lr_ref, dt_ref, so_ref, y_ref, gate_ref, pair_ref):
    for g in range(GR):
        rows = pl.ds(g * 128, 128)
        up = in_ref[:, rows]
        z = z_ref[rows, :].astype(jnp.float32).T
        sig = sigmoid(z)
        spread(y_ref, g, up * z * sig)
        so = so_ref[pl.ds(g, TT, stride=8), :]
        gate_ref[rows, :] = (up * so * sig * (1.0 + z * (1.0 - sig))).T.astype(jnp.bfloat16)
    rate2 = [-LOG2E * jnp.exp(lr_ref[8 * j:8 * j + 8, :]) for j in range(8)]

    def step(i, carry):
        t = TT - 1 - i
        here = pl.ds(pl.multiple_of(t * 8, 8), 8)
        dt = dt_ref[here, :]
        y = y_ref[here, :]
        total = carry[8] + dt
        out = []
        for j in range(8):
            c = column(c_ref[8 * j:8 * j + 8, :], t)
            out.append(jnp.exp2(dt * rate2[j]) * (c * y + carry[j]))
        return tuple(out) + (total,)

    zero = jnp.zeros((8, 128), jnp.float32)
    last = lax.fori_loop(0, TT, step, (zero,) * 9, unroll=2)
    for j in range(8):
        pair_ref[8 * j:8 * j + 8, :] = last[j]
        pair_ref[64 + 8 * j:72 + 8 * j, :] = jnp.exp2(rate2[j] * last[8])


def final_kernel(me_ref, all_ref, y_ref, ear_ref, dt_ref, us_ref, d_ref, b_ref, c_ref, lr_ref, sk_ref,
                 input_ref, delta_ref, part_ref, s1_ref, dl_ref):
    me = me_ref[0]
    rate = [jnp.exp(lr_ref[8 * j:8 * j + 8, :]) for j in range(8)]
    rate2 = [-LOG2E * rate[j] for j in range(8)]
    start = []
    for j in range(8):
        inc = jnp.zeros((8, 128), jnp.float32)
        for r in range(N_SEQ - 1, 0, -1):
            term = all_ref[r, 8 * j:8 * j + 8, :]
            decay = all_ref[r, 64 + 8 * j:72 + 8 * j, :]
            inc = jnp.where(r > me, term + decay * inc, inc)
        start.append(inc)

    def step(i, carry):
        vs, sums, sk = carry
        t = TT - 1 - i
        here = pl.ds(pl.multiple_of(t * 8, 8), 8)
        dt = dt_ref[here, :]
        y = y_ref[here, :]
        s1 = jnp.zeros((8, 128), jnp.float32)
        dl = jnp.zeros((8, 128), jnp.float32)
        nv, ns = [], []
        for j in range(8):
            b = column(b_ref[8 * j:8 * j + 8, :], t)
            c = column(c_ref[8 * j:8 * j + 8, :], t)
            adj = c * y + vs[j]
            v = jnp.exp2(dt * rate2[j]) * adj
            x = v * ear_ref[pl.ds(pl.multiple_of(t * 64, 64) + 8 * j, 8), :]
            s1 = s1 + adj * b
            dl = dl + rate[j] * x
            ns.append(sums[j] + dt * x)
            nv.append(v)
        s1_ref[here, :] = s1 + pltpu.roll(s1, 4, 0)
        dl_ref[here, :] = dl + pltpu.roll(dl, 4, 0)
        return tuple(nv), tuple(ns), sk + y * us_ref[here, :]

    zero = jnp.zeros((8, 128), jnp.float32)
    vs, sums, sk = lax.fori_loop(0, TT, step, (tuple(start), (zero,) * 8, zero), unroll=2)
    for j in range(8):
        part_ref[8 * j:8 * j + 8, :] = -rate[j] * sums[j]
    part_ref[64:72, :] = sk
    for g in range(GR):
        rows = pl.ds(g * 128, 128)
        mine = pl.ds(g, TT, stride=8)
        s1 = s1_ref[mine, :]
        inp = s1 * dt_ref[mine, :] + sk_ref[g:g + 1, :] * y_ref[mine, :]
        input_ref[rows, :] = inp.T.astype(jnp.bfloat16)
        step_grad = us_ref[mine, :] * s1 - dl_ref[mine, :]
        delta_ref[rows, :] = (step_grad.T * sigmoid(d_ref[rows, :].astype(jnp.float32))).astype(jnp.bfloat16)


MESH = pl.DeviceIdType.MESH
ANY = pl.BlockSpec(memory_space=pl.ANY)
CAP = 48


def places():
    q = lax.axis_index("seq")
    e = lax.axis_index("exp")
    return q, e


def greet(peers):
    barrier = pltpu.get_barrier_semaphore()
    for peer in peers:
        pl.semaphore_signal(barrier, inc=1, device_id=peer, device_id_type=MESH)
    pl.semaphore_wait(barrier, len(peers))


class Copies:
    def __init__(self, send, recv):
        self.send, self.recv, self.all, self.next = send, recv, [], 0

    def start(self, src, dst, peer):
        n = self.next
        self.next = n + 1
        copy = pltpu.make_async_remote_copy(
            src_ref=src, dst_ref=dst, send_sem=self.send.at[n], recv_sem=self.recv.at[n],
            device_id=peer, device_id_type=MESH,
        )
        copy.start()
        self.all.append(copy)
        return copy

    def finish(self):
        for copy in self.all:
            copy.wait_send()


def seq_at(y, c):
    return lax.rem(y + 4, 4) * 2 + c


def dispatch_kernel(s_ref, r_ref, send, recv, own_sem):
    q, e = places()
    y, c = q // 2, lax.rem(q, 2)
    qu, qd, q2, qc = seq_at(y + 1, c), seq_at(y - 1, c), seq_at(y + 2, c), y * 2 + 1 - c
    far = [(q, lax.rem(e + k, 16)) for k in range(1, 16)]
    up, down, core = (qu, e), (qd, e), (qc, e)
    greet(far + [up, down, core])
    cp = Copies(send, recv)
    own = pltpu.make_async_copy(s_ref.at[e // 2], r_ref.at[q, e], own_sem)
    own.start()
    parts = [cp.start(s_ref.at[peer[1] // 2], r_ref.at[q, e], peer) for peer in far]
    own.wait()
    for part in parts:
        part.wait_recv()
    mine = r_ref.at[q]
    a = cp.start(mine, mine, up)
    b = cp.start(mine, mine, down)
    co = [cp.start(mine, mine, core)]
    a.wait_recv()
    lo = r_ref.at[qd, pl.ds(0, 8)]
    f = cp.start(lo, lo, up)
    co.append(cp.start(r_ref.at[qd], r_ref.at[qd], core))
    b.wait_recv()
    hi = r_ref.at[qu, pl.ds(8, 8)]
    g = cp.start(hi, hi, down)
    co.append(cp.start(r_ref.at[qu], r_ref.at[qu], core))
    f.wait_recv()
    lo = r_ref.at[q2, pl.ds(0, 8)]
    co.append(cp.start(lo, lo, core))
    g.wait_recv()
    hi = r_ref.at[q2, pl.ds(8, 8)]
    co.append(cp.start(hi, hi, core))
    for copy in co:
        copy.wait_recv()
    cp.finish()


def slots_of(ids):
    lane = lax.broadcasted_iota(jnp.int32, (TT, 128), 1)
    row = lax.broadcasted_iota(jnp.int32, (TT, 128), 0)
    hits = [(ids[:, k:k + 1] == lane).astype(F32) for k in range(2)]
    lower = (lane < row).astype(F32).astype(BF16)
    before = jnp.dot(lower, (hits[0] + hits[1]).astype(BF16), preferred_element_type=F32)
    return [jnp.sum(hit * before, axis=1, keepdims=True).astype(jnp.int32) for hit in hits]


def pack_kernel(ids_ref, x_ref, g_ref, s_ref):
    ids = ids_ref[...]
    slots = slots_of(ids)
    lane = lax.broadcasted_iota(jnp.int32, (TT, 8 * CAP), 1)
    hit = jnp.zeros((TT, 8 * CAP), F32)
    for k in range(2):
        hit = hit + (ids[:, k:k + 1] * CAP + slots[k] == lane).astype(F32)
    hot = hit.T.astype(BF16)
    for a, ref in enumerate((x_ref, g_ref)):
        rows = jnp.dot(hot, ref[...], preferred_element_type=F32).astype(BF16)
        for n in range(8):
            s_ref[n, a] = rows[n * CAP:(n + 1) * CAP, :]


def expert_kernel(r_ref, wg_ref, wu_ref, wd_ref, p_ref, pr_ref, gate, up, hid, dg, du):
    i = pl.program_id(0)
    nt = (((1,), (1,)), ((), ()))

    @pl.when(i < 4)
    def _():
        x = jnp.concatenate([r_ref[:, n, 0].reshape(384, 256) for n in range(4)], axis=1)
        g = jnp.concatenate([r_ref[:, n, 1].reshape(384, 256) for n in range(4)], axis=1)
        a = jnp.dot(x, wg_ref[0], preferred_element_type=F32)
        b = jnp.dot(x, wu_ref[0], preferred_element_type=F32)
        d = lax.dot_general(g, wd_ref[0], nt, preferred_element_type=F32)

        @pl.when(i == 0)
        def _():
            gate[...] = a
            up[...] = b
            hid[...] = d

        @pl.when(i > 0)
        def _():
            gate[...] += a
            up[...] += b
            hid[...] += d

    @pl.when(i == 3)
    def _():
        v, u, h = gate[...], up[...], hid[...]
        sig = sigmoid(v)
        act = v * sig
        dg[...] = (h * u * sig * (1.0 + v * (1.0 - sig))).astype(BF16)
        gu = h * act
        du[...] = gu.astype(BF16)
        pr_ref[...] = lax.dot_general(jnp.ones((8, 512), F32), gu * u, nt, preferred_element_type=F32,
                                      precision=lax.Precision.HIGHEST)

    @pl.when(i >= 4)
    def _():
        rows = lax.dot_general(dg[...], wg_ref[0], nt, preferred_element_type=F32)
        rows = rows + lax.dot_general(du[...], wu_ref[0], nt, preferred_element_type=F32)
        for n in range(4):
            p_ref[:, n] = rows[:, n * 256:(n + 1) * 256].reshape(8, CAP, 256).astype(BF16)


def added(out, first, *others):
    total = first.astype(F32)
    for other in others:
        total = total + other.astype(F32)
    return total.astype(out)


class Ring:
    def __init__(self, cp, place, up, down, block, land):
        self.cp, self.p, self.up, self.down, self.block, self.land = cp, place, up, down, block, land

    def at(self, step, half):
        return self.block(lax.rem(self.p + step + 4, 4), half)

    def first(self):
        cp, land = self.cp, self.land
        self.u2 = cp.start(self.at(2, 0), land.at[0], self.up)
        self.d2 = cp.start(self.at(2, 1), land.at[1], self.down)
        self.uh = cp.start(self.at(1, 1), land.at[2], self.up)
        self.dl = cp.start(self.at(-1, 0), land.at[3], self.down)

    def second(self, add):
        cp, land = self.cp, self.land
        self.u2.wait_recv()
        add(land.at[6], self.at(1, 0), land.at[0])
        self.ul = cp.start(land.at[6], land.at[4], self.up)
        self.d2.wait_recv()
        add(land.at[7], self.at(-1, 1), land.at[1])
        self.dh = cp.start(land.at[7], land.at[5], self.down)

    def last(self, add, outs):
        land = self.land
        self.dl.wait_recv()
        self.ul.wait_recv()
        add(outs[0], self.at(0, 0), land.at[4], land.at[3])
        self.uh.wait_recv()
        self.dh.wait_recv()
        add(outs[1], self.at(0, 1), land.at[2], land.at[5])


def add_rows(count):
    def add(out, *refs):
        @pl.loop(0, count)
        def _(n):
            out[n] = added(out.dtype, *[ref[n] for ref in refs])
    return add


def combine_kernel(p_ref, pr_ref, t_ref, tp_ref, pair, sums, land, final, probes, mine, send, recv, own_sem):
    q, e = places()
    y, c = q // 2, lax.rem(q, 2)
    far = [(q, lax.rem(e + k, 16)) for k in range(1, 16)]
    rows = [(lax.rem(q + k, 8), e) for k in range(1, 8)]
    greet(far + rows)
    up, down, core = (seq_at(y + 1, c), e), (seq_at(y - 1, c), e), (y * 2 + 1 - c, e)
    cp = Copies(send, recv)
    order = [2, 1, 3, 0]
    halves = []
    for n in order:
        other = lax.rem(y + n, 4)
        halves.append(cp.start(p_ref.at[other * 2 + 1 - c], pair.at[other], core))
    tells = [cp.start(pr_ref, probes.at[k], rows[k]) for k in range(7)]
    add = add_rows(8)

    def block(d, half):
        return sums.at[d, pl.ds(8 * half, 8)]

    for n, copy in zip(order, halves):
        other = lax.rem(y + n, 4)
        copy.wait_recv()
        add_rows(16)(sums.at[other], p_ref.at[other * 2 + c], pair.at[other])
    ring = Ring(cp, y, up, down, block, land)
    ring.first()
    for tell in tells:
        tell.wait_recv()
    total = pr_ref[...]
    for k in range(7):
        total = total + probes[k]
    mine[...] = pltpu.roll(total, lax.rem(8 - q, 8) * CAP, 1)[:, :128]
    ring.second(add)
    own_probe = pltpu.make_async_copy(mine, tp_ref.at[e], own_sem.at[0])
    own_probe.start()
    shares = [cp.start(mine, tp_ref.at[e], peer) for peer in far]
    ring.last(add, (final.at[pl.ds(0, 8)], final.at[pl.ds(8, 8)]))
    own = pltpu.make_async_copy(final.at[e], t_ref.at[e], own_sem.at[1])
    own.start()
    shares += [cp.start(final.at[peer[1]], t_ref.at[e], peer) for peer in far]
    own_probe.wait()
    own.wait()
    for share in shares:
        share.wait_recv()
    cp.finish()


def resid_kernel(ids_ref, w_ref, t_ref, tp_ref, g_ref, ow_ref, res_ref, probs_ref, i_ref, held):
    @pl.when(pl.program_id(0) == 0)
    def _():
        ids = ids_ref[...]
        slots = slots_of(ids)
        lane = lax.broadcasted_iota(jnp.int32, (TT, 8 * CAP), 1)
        near = lax.broadcasted_iota(jnp.int32, (TT, 128), 1)
        total = g_ref[...].astype(F32)
        even = jnp.concatenate([t_ref[2 * n] for n in range(8)], axis=0)
        odd = jnp.concatenate([t_ref[2 * n + 1] for n in range(8)], axis=0)
        probs = []
        for k in range(2):
            hot = (ids[:, k:k + 1] * CAP + slots[k] == lane).astype(F32).astype(BF16)
            route = jnp.dot(hot, even, preferred_element_type=F32) + jnp.dot(hot, odd, preferred_element_type=F32)
            total = total + w_ref[:, k:k + 1] * route
            acc = jnp.zeros((TT, 128), F32)
            for n in range(8):
                row = tp_ref[2 * n, 0:1, :] + tp_ref[2 * n + 1, 0:1, :]
                hit = (ids[:, k:k + 1] == n) & (slots[k] == near)
                acc = acc + jnp.where(hit, row, 0.0)
            probs.append(jnp.sum(acc, axis=1, keepdims=True))
        held[...] = total.astype(BF16)
        res_ref[...] = held[...]
        probs_ref[...] = jnp.concatenate(probs, axis=1)

    nt = (((1,), (1,)), ((), ()))
    part = lax.dot_general(held[...], ow_ref[...], nt, preferred_element_type=F32)
    for n in range(4):
        i_ref[0, n] = part[:, n * 512:(n + 1) * 512].astype(BF16)


def spread_kernel(i_ref, in_ref, lx, lz, kx, kz, jx, jz, send, recv):
    q, e = places()
    x, z = e // 4, lax.rem(e, 4)
    xu, xd = (q, lax.rem(x + 1, 4) * 4 + z), (q, lax.rem(x + 3, 4) * 4 + z)
    zu, zd = (q, x * 4 + lax.rem(z + 1, 4)), (q, x * 4 + lax.rem(z + 3, 4))
    greet([xu, xd, zu, zd])
    cp = Copies(send, recv)
    rx = Ring(cp, x, xu, xd, lambda d, half: i_ref.at[d, pl.ds(2 * half, 2), pl.ds(0, 64)], lx)
    rz = Ring(cp, z, zu, zd, lambda d, half: i_ref.at[pl.ds(2 * half, 2), d, pl.ds(64, 64)], lz)
    two = add_rows(2)
    rx.first()
    rz.first()
    rx.second(two)
    rz.second(two)
    rx.last(two, (jx.at[pl.ds(0, 2)], jx.at[pl.ds(2, 2)]))
    sx = Ring(cp, z, zu, zd, lambda d, half: jx.at[d, pl.ds(32 * half, 32)], kx)
    sx.first()
    rz.last(two, (jz.at[pl.ds(0, 2)], jz.at[pl.ds(2, 2)]))
    sz = Ring(cp, x, xu, xd, lambda d, half: jz.at[d, pl.ds(32 * half, 32)], kz)
    sz.first()

    def one(out, *refs):
        out[...] = added(out.dtype, *[ref[...] for ref in refs])

    sx.second(one)
    sz.second(one)
    sx.last(one, (in_ref.at[pl.ds(0, 32)], in_ref.at[pl.ds(32, 32)]))
    sz.last(one, (in_ref.at[pl.ds(64, 32)], in_ref.at[pl.ds(96, 32)]))
    cp.finish()


def gather_kernel(pair_ref, all_ref, send, recv, own_sem):
    q, e = places()
    rows = [(lax.rem(q + k, 8), e) for k in range(1, 8)]
    greet(rows)
    cp = Copies(send, recv)
    own = pltpu.make_async_copy(pair_ref, all_ref.at[q], own_sem)
    own.start()
    parts = [cp.start(pair_ref, all_ref.at[q], peer) for peer in rows]
    own.wait()
    for part in parts:
        part.wait_recv()
    cp.finish()


def total_kernel(part_ref, out_ref, land, send, recv):
    q, e = places()
    rows = [(lax.rem(q + k, 8), e) for k in range(1, 8)]
    greet(rows)
    cp = Copies(send, recv)
    parts = [cp.start(part_ref, land.at[q], peer) for peer in rows]
    land[q] = part_ref[...]
    for part in parts:
        part.wait_recv()
    total = land[0]
    for k in range(1, 8):
        total = total + land[k]
    out_ref[...] = total
    cp.finish()


def sems(count):
    return [pltpu.SemaphoreType.DMA((count,))] * 2


def talk(number, limit=None):
    return pltpu.CompilerParams(collective_id=number, has_side_effects=True, vmem_limit_bytes=limit)


def local(
    moe_input,
    out_grad,
    expert_ids,
    expert_route_weights,
    gate_weight,
    up_weight,
    down_weight,
    out_weight,
    scan_input,
    delta_raw,
    mixer_gate_branch,
    state_input,
    state_output,
    log_rates,
    skip_gain,
    block_states,
):
    b_rep = jnp.repeat(state_input, GR, axis=0)
    c_rep = jnp.repeat(state_output, GR, axis=0)
    rates = log_rates.reshape(64, 128)
    start = block_states.reshape(64, 128)
    skip = jnp.tile(skip_gain.reshape(GR, 128), (2, 1))
    packed = pl.pallas_call(
        pack_kernel,
        out_shape=shape((8, 2, CAP, 256), BF16),
        in_specs=[VMEM] * 3,
        out_specs=VMEM,
        name="pack_rows",
    )(expert_ids, moe_input, out_grad)
    rows = pl.pallas_call(
        dispatch_kernel,
        out_shape=shape((8, 16, 2, CAP, 256), BF16),
        in_specs=[ANY],
        out_specs=ANY,
        scratch_shapes=sems(24) + [pltpu.SemaphoreType.DMA],
        compiler_params=talk(1),
        name="dispatch",
    )(packed)
    parts, probes = pl.pallas_call(
        expert_kernel,
        grid=(8,),
        out_shape=(shape((8, 16, CAP, 256), BF16), shape((8, 384))),
        in_specs=[
            pl.BlockSpec((8, 4, 2, CAP, 256), lambda i: (0, jnp.minimum(i, 3), 0, 0, 0)),
            pl.BlockSpec((1, 1024, 512), lambda i: (0, lax.rem(i, 4), 0)),
            pl.BlockSpec((1, 1024, 512), lambda i: (0, lax.rem(i, 4), 0)),
            pl.BlockSpec((1, 512, 1024), lambda i: (0, 0, jnp.minimum(i, 3))),
        ],
        out_specs=(
            pl.BlockSpec((8, 4, CAP, 256), lambda i: (0, jnp.maximum(i - 4, 0), 0, 0)),
            pl.BlockSpec((8, 384), lambda i: (0, 0)),
        ),
        scratch_shapes=[pltpu.VMEM((384, 512), F32)] * 3 + [pltpu.VMEM((384, 512), BF16)] * 2,
        name="experts",
    )(rows, gate_weight, up_weight, down_weight)
    returned, told = pl.pallas_call(
        combine_kernel,
        out_shape=(shape((16, CAP, 256), BF16), shape((16, 8, 128))),
        in_specs=[VMEM] * 2,
        out_specs=(VMEM,) * 2,
        scratch_shapes=[
            pltpu.VMEM((4, 16, CAP, 256), BF16),
            pltpu.VMEM((4, 16, CAP, 256), BF16),
            pltpu.VMEM((8, 8, CAP, 256), BF16),
            pltpu.VMEM((16, CAP, 256), BF16),
            pltpu.VMEM((7, 8, 384), F32),
            pltpu.VMEM((8, 128), F32),
        ] + sems(47) + [pltpu.SemaphoreType.DMA((2,))],
        compiler_params=talk(2),
        name="combine",
    )(parts, probes)
    resid_grad, probs_grad, inner_parts = pl.pallas_call(
        resid_kernel,
        grid=(4,),
        out_shape=(shape((TT, 256), BF16), shape((TT, 2)), shape((4, 4, TT, 512), BF16)),
        in_specs=[
            pl.BlockSpec((TT, 2), lambda i: (0, 0)),
            pl.BlockSpec((TT, 2), lambda i: (0, 0)),
            pl.BlockSpec((16, CAP, 256), lambda i: (0, 0, 0)),
            pl.BlockSpec((16, 8, 128), lambda i: (0, 0, 0)),
            pl.BlockSpec((TT, 256), lambda i: (0, 0)),
            pl.BlockSpec((2048, 256), lambda i: (i, 0)),
        ],
        out_specs=(
            pl.BlockSpec((TT, 256), lambda i: (0, 0)),
            pl.BlockSpec((TT, 2), lambda i: (0, 0)),
            pl.BlockSpec((1, 4, TT, 512), lambda i: (i, 0, 0, 0)),
        ),
        scratch_shapes=[pltpu.VMEM((TT, 256), BF16)],
        name="resid_and_inner",
    )(expert_ids, expert_route_weights, returned, told, out_grad, out_weight)
    inner_grad = pl.pallas_call(
        spread_kernel,
        out_shape=shape((TT, 512)),
        in_specs=[VMEM],
        out_specs=VMEM,
        scratch_shapes=[pltpu.VMEM((8, 2, 64, 512), BF16)] * 2 + [pltpu.VMEM((8, 32, 512), F32)] * 2
        + [pltpu.VMEM((4, 64, 512), F32)] * 2 + sems(24),
        compiler_params=talk(3),
        name="inner_sum",
    )(inner_parts)
    earlier, steps, signal, scan_out = pl.pallas_call(
        forward_kernel,
        out_shape=(shape((TT * 64, 128)), shape((TT * 8, 128)), shape((TT * 8, 128)), shape((TT * 8, 128))),
        in_specs=[VMEM] * 7,
        out_specs=(VMEM,) * 4,
        name="scan_forward",
    )(scan_input, delta_raw, b_rep, c_rep, rates, start, skip)
    y_grad, gate_grad, pair = pl.pallas_call(
        middle_kernel,
        out_shape=(shape((TT * 8, 128)), shape((512, 128), BF16), shape((128, 128))),
        in_specs=[VMEM] * 6,
        out_specs=(VMEM,) * 3,
        name="adjoint_summary",
    )(inner_grad, mixer_gate_branch, c_rep, rates, steps, scan_out)
    pairs = pl.pallas_call(
        gather_kernel,
        out_shape=shape((8, 128, 128)),
        in_specs=[VMEM],
        out_specs=VMEM,
        scratch_shapes=sems(7) + [pltpu.SemaphoreType.DMA],
        compiler_params=talk(4),
        name="carry_gather",
    )(pair)
    me = lax.axis_index("seq").astype(jnp.int32).reshape(1)
    input_grad, delta_grad, part = pl.pallas_call(
        final_kernel,
        out_shape=(shape((512, 128), BF16), shape((512, 128), BF16), shape((72, 128))),
        in_specs=[SMEM] + [VMEM] * 10,
        out_specs=(VMEM,) * 3,
        scratch_shapes=[pltpu.VMEM((TT * 8, 128), F32)] * 2,
        name="adjoint_final",
    )(me, pairs, y_grad, earlier, steps, signal, delta_raw, b_rep, c_rep, rates, skip)
    total = pl.pallas_call(
        total_kernel,
        out_shape=shape((72, 128)),
        in_specs=[VMEM],
        out_specs=VMEM,
        scratch_shapes=[pltpu.VMEM((8, 72, 128), F32)] + sems(7),
        compiler_params=talk(5),
        name="token_sums",
    )(part)
    rates_grad = total[:64].reshape(16, 512)
    skip_grad = total[64:68].reshape(512)
    return (resid_grad, probs_grad, input_grad, delta_grad, gate_grad, rates_grad, skip_grad)


def solution(mesh):
    in_specs = (
        P("seq", "exp"),
        P("seq", "exp"),
        P("seq", None),
        P("seq", None),
        P("exp", None, "seq"),
        P("exp", None, "seq"),
        P("exp", "seq", None),
        P(None, "exp"),
        P("exp", "seq"),
        P("exp", "seq"),
        P("exp", "seq"),
        P(None, "seq"),
        P(None, "seq"),
        P(None, "exp"),
        P("exp"),
        P("seq", None, "exp"),
    )
    out_specs = (
        P("seq", "exp"),
        P("seq", None),
        P("exp", "seq"),
        P("exp", "seq"),
        P("exp", "seq"),
        P(None, "exp"),
        P("exp"),
    )
    return jax.shard_map(local, mesh=mesh, in_specs=in_specs, out_specs=out_specs, check_vma=False)
```

```python
import jax
import jax.numpy as jnp
from jax import lax
from jax.experimental import pallas as pl
from jax.experimental.pallas import tpu as pltpu
from jax.sharding import PartitionSpec as P

N_SEQ = 8
F32 = jnp.float32
BF16 = jnp.bfloat16
VMEM = pl.BlockSpec(memory_space=pltpu.VMEM)
SMEM = pl.BlockSpec(memory_space=pltpu.SMEM)


def shape(dims, kind=jnp.float32):
    return jax.ShapeDtypeStruct(dims, kind)


LOG2E = 1.4426950408889634
GR = 4
TT = 128
ROWS = 64


def softplus(v):
    return jnp.maximum(v, 0.0) + jnp.log1p(jnp.exp(-jnp.abs(v)))


def sigmoid(v):
    return 1.0 / (1.0 + jnp.exp(-v))


def spread(ref, g, val):
    ref[pl.ds(g, TT, stride=8), :] = val
    ref[pl.ds(GR + g, TT, stride=8), :] = val


def column(rep, t):
    return jnp.take_along_axis(rep, jnp.full((8, 128), t, jnp.int32), axis=1)


def grouped(ref, j):
    return jnp.concatenate(
        [ref[2 * j + p:2 * j + p + 1, g * 128:(g + 1) * 128] for p in range(2) for g in range(GR)], axis=0)


def doubled(ref, j):
    return jnp.concatenate(
        [jnp.broadcast_to(ref[2 * j + p:2 * j + p + 1, :], (GR, 128)) for p in range(2)], axis=0)


def octet(j):
    return slice(8 * j, 8 * j + 8)


def at_token(t):
    return pl.ds(pl.multiple_of(t * 8, 8), 8)


def at_state(t, j):
    return pl.ds(pl.multiple_of(t * ROWS, ROWS) + 8 * j, 8)


class Forward:
    def __init__(self, u, d, b, c, lr, st, sk, rate, decay, skip, a, ear, bb, cb, dt, us, so):
        self.__dict__.update(locals())

    def open(self):
        for g in range(GR):
            rows = pl.ds(g * 128, 128)
            spread(self.dt, g, softplus(self.d[rows, :].astype(F32).T))
            spread(self.us, g, self.u[rows, :].astype(F32).T)
        for j in range(8):
            self.rate[octet(j), :] = jnp.exp(grouped(self.lr, j))
        self.skip[...] = jnp.concatenate(
            [self.sk[0:1, g * 128:(g + 1) * 128] for p in range(2) for g in range(GR)], axis=0)
        one = jnp.ones((8, 128), F32)
        return tuple(grouped(self.st.at[0], j) for j in range(8)) + (one,) * 8

    def run(self, first, last, carry):
        rate2 = [-LOG2E * self.rate[octet(j), :] for j in range(8)]
        b_rep = [doubled(self.b, j) for j in range(8)]
        c_rep = [doubled(self.c, j) for j in range(8)]
        skip = self.skip[...]

        def step(t, carry):
            here = at_token(t)
            dt = self.dt[here, :]
            u = self.us[here, :]
            du = dt * u
            acc = jnp.zeros((8, 128), F32)
            states, products = [], []
            for j in range(8):
                spot = at_state(t, j)
                b = column(b_rep[j], t)
                c = column(c_rep[j], t)
                a = jnp.exp2(dt * rate2[j])
                state = a * carry[j] + du * b
                self.ear[spot, :] = carry[j]
                self.a[spot, :] = a
                self.bb[spot, :] = b
                self.cb[spot, :] = c
                acc = acc + c * state
                states.append(state)
                products.append(carry[8 + j] * a)
            self.so[here, :] = acc + pltpu.roll(acc, 4, 0) + skip * u
            return tuple(states + products)

        return lax.fori_loop(first, last, step, carry)

    def close(self, carry):
        for j in range(8):
            self.decay[octet(j), :] = carry[8 + j]


MESH = pl.DeviceIdType.MESH
ANY = pl.BlockSpec(memory_space=pl.ANY)
CAP = 48


def places():
    q = lax.axis_index("seq")
    e = lax.axis_index("exp")
    return q, e


def greet(peers):
    barrier = pltpu.get_barrier_semaphore()
    for peer in peers:
        pl.semaphore_signal(barrier, inc=1, device_id=peer, device_id_type=MESH)
    pl.semaphore_wait(barrier, len(peers))


class Copies:
    def __init__(self, send, recv):
        self.send, self.recv, self.all, self.next = send, recv, [], 0

    def make(self, src, dst, peer):
        n = self.next
        self.next = n + 1
        return pltpu.make_async_remote_copy(
            src_ref=src, dst_ref=dst, send_sem=self.send.at[n], recv_sem=self.recv.at[n],
            device_id=peer, device_id_type=MESH,
        )

    def start(self, src, dst, peer):
        copy = self.make(src, dst, peer)
        copy.start()
        self.all.append(copy)
        return copy

    def finish(self):
        for copy in self.all:
            copy.wait_send()


def seq_at(y, c):
    return lax.rem(y + 4, 4) * 2 + c


def dispatch_kernel(s_ref, u, d, b_ref, c_ref, lr, st, sk, r_ref, a_h, ear_h, bb_h, cb_h, dt_h, us_h, so_h, rate, decay, skip,
                    a_v, ear, bb, cb, dt, us, so, send, recv, own_sem, near):
    q, e = places()
    y, c = q // 2, lax.rem(q, 2)
    qu, qd, q2, qc = seq_at(y + 1, c), seq_at(y - 1, c), seq_at(y + 2, c), y * 2 + 1 - c
    far = [(q, lax.rem(e + k, 16)) for k in range(1, 16)]
    up, down, core = (qu, e), (qd, e), (qc, e)
    greet(far + [up, down, core])
    cp = Copies(send, recv)
    own = pltpu.make_async_copy(s_ref.at[e // 2], r_ref.at[q, e], own_sem)
    own.start()
    parts = [cp.start(s_ref.at[peer[1] // 2], r_ref.at[q, e], peer) for peer in far]
    scan = Forward(u, d, b_ref, c_ref, lr, st, sk, rate, decay, skip, a_v, ear, bb, cb, dt, us, so)
    carry = scan.run(0, 64, scan.open())
    own.wait()
    for part in parts:
        part.wait_recv()
    mine = r_ref.at[q]
    a = cp.start(mine, mine, up)
    b = cp.start(mine, mine, down)
    co = [cp.start(mine, mine, core)]
    scan.close(scan.run(64, TT, carry))
    saves = [pltpu.make_async_copy(src, dst, near.at[n]) for n, (src, dst) in enumerate(
        ((a_v, a_h), (ear, ear_h), (bb, bb_h), (cb, cb_h), (dt, dt_h), (us, us_h), (so, so_h)))]
    for save in saves:
        save.start()
    a.wait_recv()
    lo = r_ref.at[qd, pl.ds(0, 8)]
    f = cp.start(lo, lo, up)
    co.append(cp.start(r_ref.at[qd], r_ref.at[qd], core))
    b.wait_recv()
    hi = r_ref.at[qu, pl.ds(8, 8)]
    g = cp.start(hi, hi, down)
    co.append(cp.start(r_ref.at[qu], r_ref.at[qu], core))
    f.wait_recv()
    lo = r_ref.at[q2, pl.ds(0, 8)]
    co.append(cp.start(lo, lo, core))
    g.wait_recv()
    hi = r_ref.at[q2, pl.ds(8, 8)]
    co.append(cp.start(hi, hi, core))
    for copy in co:
        copy.wait_recv()
    for save in saves:
        save.wait()
    cp.finish()


def slots_of(ids):
    lane = lax.broadcasted_iota(jnp.int32, (TT, 128), 1)
    row = lax.broadcasted_iota(jnp.int32, (TT, 128), 0)
    hits = [(ids[:, k:k + 1] == lane).astype(F32) for k in range(2)]
    lower = (lane < row).astype(F32).astype(BF16)
    before = jnp.dot(lower, (hits[0] + hits[1]).astype(BF16), preferred_element_type=F32)
    return [jnp.sum(hit * before, axis=1, keepdims=True).astype(jnp.int32) for hit in hits]


def pack_kernel(ids_ref, x_ref, g_ref, s_ref):
    ids = ids_ref[...]
    slots = slots_of(ids)
    lane = lax.broadcasted_iota(jnp.int32, (TT, 8 * CAP), 1)
    hit = jnp.zeros((TT, 8 * CAP), F32)
    for k in range(2):
        hit = hit + (ids[:, k:k + 1] * CAP + slots[k] == lane).astype(F32)
    hot = hit.T.astype(BF16)
    for a, ref in enumerate((x_ref, g_ref)):
        rows = jnp.dot(hot, ref[...], preferred_element_type=F32).astype(BF16)
        for n in range(8):
            s_ref[n, a] = rows[n * CAP:(n + 1) * CAP, :]


def expert_kernel(r_ref, wg_ref, wu_ref, wd_ref, p_ref, pr_ref, gate, up, hid, dg, du):
    i = pl.program_id(0)
    nt = (((1,), (1,)), ((), ()))

    @pl.when(i < 4)
    def _():
        x = jnp.concatenate([r_ref[:, n, 0].reshape(384, 256) for n in range(4)], axis=1)
        g = jnp.concatenate([r_ref[:, n, 1].reshape(384, 256) for n in range(4)], axis=1)
        a = jnp.dot(x, wg_ref[0], preferred_element_type=F32)
        b = jnp.dot(x, wu_ref[0], preferred_element_type=F32)
        d = lax.dot_general(g, wd_ref[0], nt, preferred_element_type=F32)

        @pl.when(i == 0)
        def _():
            gate[...] = a
            up[...] = b
            hid[...] = d

        @pl.when(i > 0)
        def _():
            gate[...] += a
            up[...] += b
            hid[...] += d

    @pl.when(i == 3)
    def _():
        v, u, h = gate[...], up[...], hid[...]
        sig = sigmoid(v)
        act = v * sig
        dg[...] = (h * u * sig * (1.0 + v * (1.0 - sig))).astype(BF16)
        gu = h * act
        du[...] = gu.astype(BF16)
        pr_ref[...] = lax.dot_general(jnp.ones((8, 512), F32), gu * u, nt, preferred_element_type=F32,
                                      precision=lax.Precision.HIGHEST)

    @pl.when(i >= 4)
    def _():
        rows = lax.dot_general(dg[...], wg_ref[0], nt, preferred_element_type=F32)
        rows = rows + lax.dot_general(du[...], wu_ref[0], nt, preferred_element_type=F32)
        for n in range(4):
            p_ref[:, n] = rows[:, n * 256:(n + 1) * 256].reshape(8, CAP, 256).astype(BF16)


def added(out, first, *others):
    total = first.astype(F32)
    for other in others:
        total = total + other.astype(F32)
    return total.astype(out)


class Ring:
    def __init__(self, cp, place, up, down, block, land):
        self.cp, self.p, self.up, self.down, self.block, self.land = cp, place, up, down, block, land

    def at(self, step, half, own=1):
        return self.block(lax.rem(self.p + step + 4, 4), half)[own]

    def first(self):
        cp, land = self.cp, self.land
        self.u2 = cp.start(self.at(2, 0, 0), land.at[0], self.up)
        self.d2 = cp.start(self.at(2, 1, 0), land.at[1], self.down)
        self.uh = cp.start(self.at(1, 1, 0), land.at[2], self.up)
        self.dl = cp.start(self.at(-1, 0, 0), land.at[3], self.down)

    def second(self, add):
        cp, land = self.cp, self.land
        self.u2.wait_recv()
        add(land.at[6], self.at(1, 0), land.at[0])
        self.ul = cp.start(land.at[6], land.at[4], self.up)
        self.d2.wait_recv()
        add(land.at[7], self.at(-1, 1), land.at[1])
        self.dh = cp.start(land.at[7], land.at[5], self.down)

    def last(self, add, outs):
        land = self.land
        self.dl.wait_recv()
        self.ul.wait_recv()
        add(outs[0], self.at(0, 0), land.at[4], land.at[3])
        self.uh.wait_recv()
        self.dh.wait_recv()
        add(outs[1], self.at(0, 1), land.at[2], land.at[5])


def add_rows(count):
    def add(out, *refs):
        @pl.loop(0, count)
        def _(n):
            out[n] = added(out.dtype, *[ref[n] for ref in refs])
    return add


def combine_kernel(p_ref, pr_ref, t_ref, tp_ref, pair, sums, land, final, probes, mine, send, recv, own_sem):
    q, e = places()
    y, c = q // 2, lax.rem(q, 2)
    far = [(q, lax.rem(e + k, 16)) for k in range(1, 16)]
    rows = [(lax.rem(q + k, 8), e) for k in range(1, 8)]
    greet(far + rows)
    up, down, core = (seq_at(y + 1, c), e), (seq_at(y - 1, c), e), (y * 2 + 1 - c, e)
    cp = Copies(send, recv)
    order = [2, 1, 3, 0]
    halves = []
    for n in order:
        other = lax.rem(y + n, 4)
        halves.append(cp.start(p_ref.at[other * 2 + 1 - c], pair.at[other], core))
    tells = [cp.start(pr_ref, probes.at[k], rows[k]) for k in range(7)]
    add = add_rows(8)

    def block(d, half):
        return (sums.at[d, pl.ds(8 * half, 8)],) * 2

    for n, copy in zip(order, halves):
        other = lax.rem(y + n, 4)
        copy.wait_recv()
        add_rows(16)(sums.at[other], p_ref.at[other * 2 + c], pair.at[other])
    ring = Ring(cp, y, up, down, block, land)
    ring.first()
    for tell in tells:
        tell.wait_recv()
    total = pr_ref[...]
    for k in range(7):
        total = total + probes[k]
    mine[...] = pltpu.roll(total, lax.rem(8 - q, 8) * CAP, 1)[:, :128]
    ring.second(add)
    own_probe = pltpu.make_async_copy(mine, tp_ref.at[e], own_sem.at[0])
    own_probe.start()
    shares = [cp.start(mine, tp_ref.at[e], peer) for peer in far]
    ring.last(add, (final.at[pl.ds(0, 8)], final.at[pl.ds(8, 8)]))
    own = pltpu.make_async_copy(final.at[e], t_ref.at[e], own_sem.at[1])
    own.start()
    shares += [cp.start(final.at[peer[1]], t_ref.at[e], peer) for peer in far]
    own_probe.wait()
    own.wait()
    for share in shares:
        share.wait_recv()
    cp.finish()


def resid_kernel(ids_ref, w_ref, t_ref, tp_ref, g_ref, ow_ref, res_ref, probs_ref, i_ref, held):
    @pl.when(pl.program_id(0) == 0)
    def _():
        ids = ids_ref[...]
        slots = slots_of(ids)
        lane = lax.broadcasted_iota(jnp.int32, (TT, 8 * CAP), 1)
        near = lax.broadcasted_iota(jnp.int32, (TT, 128), 1)
        total = g_ref[...].astype(F32)
        even = jnp.concatenate([t_ref[2 * n] for n in range(8)], axis=0)
        odd = jnp.concatenate([t_ref[2 * n + 1] for n in range(8)], axis=0)
        probs = []
        for k in range(2):
            hot = (ids[:, k:k + 1] * CAP + slots[k] == lane).astype(F32).astype(BF16)
            route = jnp.dot(hot, even, preferred_element_type=F32) + jnp.dot(hot, odd, preferred_element_type=F32)
            total = total + w_ref[:, k:k + 1] * route
            acc = jnp.zeros((TT, 128), F32)
            for n in range(8):
                row = tp_ref[2 * n, 0:1, :] + tp_ref[2 * n + 1, 0:1, :]
                hit = (ids[:, k:k + 1] == n) & (slots[k] == near)
                acc = acc + jnp.where(hit, row, 0.0)
            probs.append(jnp.sum(acc, axis=1, keepdims=True))
        held[...] = total.astype(BF16)
        res_ref[...] = held[...]
        probs_ref[...] = jnp.concatenate(probs, axis=1)

    nt = (((1,), (1,)), ((), ()))
    part = lax.dot_general(held[...], ow_ref[...], nt, preferred_element_type=F32)
    for n in range(4):
        i_ref[0, n] = part[:, n * 512:(n + 1) * 512].astype(BF16)


def sems(count):
    return [pltpu.SemaphoreType.DMA((count,))] * 2


def talk(number, limit=None):
    return pltpu.CompilerParams(collective_id=number, has_side_effects=True, vmem_limit_bytes=limit)


def tail_kernel(i_ref, a_h, ear_h, bb_h, cb_h, dt_h, us_h, so_h, z_ref, d_ref, rate_ref, decay_ref, skip_ref,
                gate_ref, input_ref, delta_ref, rates_ref, skipped_ref,
                ivm, lx, lz, kx, kz, jx, jz, inner, a, ear, bb, cb, dt, us, so, ys, s1s, dls,
                term, terms, decays, part, other, both, three, send, recv, near):
    q, e = places()
    x, z = e // 4, lax.rem(e, 4)
    y, c = q // 2, lax.rem(q, 2)
    xu, xd = (q, lax.rem(x + 1, 4) * 4 + z), (q, lax.rem(x + 3, 4) * 4 + z)
    zu, zd = (q, x * 4 + lax.rem(z + 1, 4)), (q, x * 4 + lax.rem(z + 3, 4))
    loads = [pltpu.make_async_copy(src, dst, near.at[n]) for n, (src, dst) in enumerate(
        ((i_ref, ivm), (dt_h, dt), (us_h, us), (so_h, so), (a_h, a), (cb_h, cb), (ear_h, ear), (bb_h, bb)))]
    for load in loads:
        load.start()
    terms[...] = jnp.zeros_like(terms)
    decays[...] = jnp.zeros_like(decays)
    greet([xu, xd, zu, zd] + [(lax.rem(q + k, 8), e) for k in range(1, 8)])
    cp = Copies(send, recv)

    def earlier_shards(src, land):
        copies = []
        for k in range(1, 8):
            copy = cp.make(src, land.at[k - 1], (lax.rem(q + 8 - k, 8), e))

            @pl.when(q >= k)
            def _(copy=copy):
                copy.start()
            copies.append(copy)

        def arrive():
            for k in range(1, 8):
                @pl.when(q + k < 8)
                def _(k=k):
                    copies[k - 1].wait_recv()

        def leave():
            for k in range(1, 8):
                @pl.when(q >= k)
                def _(k=k):
                    copies[k - 1].wait_send()
        return arrive, leave

    rx = Ring(cp, x, xu, xd, lambda d, half: (i_ref.at[d, pl.ds(2 * half, 2), pl.ds(0, 64)],
                                              ivm.at[d, pl.ds(2 * half, 2), pl.ds(0, 64)]), lx)
    rz = Ring(cp, z, zu, zd, lambda d, half: (i_ref.at[pl.ds(2 * half, 2), d, pl.ds(64, 64)],
                                              ivm.at[pl.ds(2 * half, 2), d, pl.ds(64, 64)]), lz)
    two = add_rows(2)
    rx.first()
    rz.first()
    decays_in, decays_out = earlier_shards(decay_ref, decays)
    loads[0].wait()
    rx.second(two)
    rz.second(two)
    rx.last(two, (jx.at[pl.ds(0, 2)], jx.at[pl.ds(2, 2)]))
    sx = Ring(cp, z, zu, zd, lambda d, half: (jx.at[d, pl.ds(32 * half, 32)],) * 2, kx)
    sx.first()
    rz.last(two, (jz.at[pl.ds(0, 2)], jz.at[pl.ds(2, 2)]))
    sz = Ring(cp, x, xu, xd, lambda d, half: (jz.at[d, pl.ds(32 * half, 32)],) * 2, kz)
    sz.first()

    def one(out, *refs):
        out[...] = added(out.dtype, *[ref[...] for ref in refs])

    sx.second(one)
    sz.second(one)
    sx.last(one, (inner.at[pl.ds(0, 32)], inner.at[pl.ds(32, 32)]))
    sz.last(one, (inner.at[pl.ds(64, 32)], inner.at[pl.ds(96, 32)]))
    for load in loads[1:]:
        load.wait()

    for g in range(GR):
        rows = pl.ds(g * 128, 128)
        act = z_ref[rows, :].astype(F32).T
        spread(ys, g, inner[:, rows] * act * sigmoid(act))

    zero = jnp.zeros((8, 128), F32)

    def summary(i, carry):
        t = TT - 1 - i
        grad = ys[at_token(t), :]
        return tuple(a[at_state(t, j), :] * (cb[at_state(t, j), :] * grad + carry[j]) for j in range(8))

    last = lax.fori_loop(0, TT, summary, (zero,) * 8, unroll=4)
    for j in range(8):
        term[octet(j), :] = last[j]
    terms_in, terms_out = earlier_shards(term, terms)

    for g in range(GR):
        rows = pl.ds(g * 128, 128)
        act = z_ref[rows, :].astype(F32).T
        sig = sigmoid(act)
        gated = inner[:, rows] * so[pl.ds(g, TT, stride=8), :] * sig * (1.0 + act * (1.0 - sig))
        gate_ref[rows, :] = gated.T.astype(BF16)

    decays_in()
    terms_in()
    rate = [rate_ref[octet(j), :] for j in range(8)]
    start = []
    for j in range(8):
        inc = zero
        for k in range(7, 0, -1):
            inc = terms[k - 1, octet(j), :] + decays[k - 1, octet(j), :] * inc
        start.append(inc)

    def step(i, carry):
        vs, sums, sk = carry
        t = TT - 1 - i
        here = at_token(t)
        grad = ys[here, :]
        size = dt[here, :]
        s1, dl = zero, zero
        nv, ns = [], []
        for j in range(8):
            spot = at_state(t, j)
            adj = cb[spot, :] * grad + vs[j]
            v = a[spot, :] * adj
            w = v * ear[spot, :]
            s1 = s1 + adj * bb[spot, :]
            dl = dl + rate[j] * w
            ns.append(sums[j] + size * w)
            nv.append(v)
        s1s[here, :] = s1 + pltpu.roll(s1, 4, 0)
        dls[here, :] = dl + pltpu.roll(dl, 4, 0)
        return tuple(nv), tuple(ns), sk + grad * us[here, :]

    vs, sums, sk = lax.fori_loop(0, TT, step, (tuple(start), (zero,) * 8, zero), unroll=2)
    for j in range(8):
        part[octet(j), :] = -rate[j] * sums[j]
    part[64:72, :] = sk
    swap = cp.start(part, other, (y * 2 + 1 - c, e))

    for g in range(GR):
        rows = pl.ds(g * 128, 128)
        mine = pl.ds(g, TT, stride=8)
        s1 = s1s[mine, :]
        inp = s1 * dt[mine, :] + skip_ref[g:g + 1, :] * ys[mine, :]
        input_ref[rows, :] = inp.T.astype(BF16)

    swap.wait_recv()
    both[...] = part[...] + other[...]
    shares = [cp.start(both, three.at[k - 1], (seq_at(y + k, c), e)) for k in range(1, 4)]

    for g in range(GR):
        rows = pl.ds(g * 128, 128)
        mine = pl.ds(g, TT, stride=8)
        step_grad = us[mine, :] * s1s[mine, :] - dls[mine, :]
        delta_ref[rows, :] = (step_grad.T * sigmoid(d_ref[rows, :].astype(F32))).astype(BF16)

    for share in shares:
        share.wait_recv()
    both2 = both[...] + three[0] + three[1] + three[2]
    for j in range(8):
        for p in range(2):
            for g in range(GR):
                row = 8 * j + GR * p + g
                rates_ref[2 * j + p:2 * j + p + 1, g * 128:(g + 1) * 128] = both2[row:row + 1, :]
    for g in range(GR):
        skipped_ref[0:1, g * 128:(g + 1) * 128] = both2[64 + g:65 + g, :]
    decays_out()
    terms_out()
    cp.finish()


def finish_kernel(*refs):
    for src, dst in zip(refs[:5], refs[5:]):
        dst[...] = src[...]


def local(
    moe_input,
    out_grad,
    expert_ids,
    expert_route_weights,
    gate_weight,
    up_weight,
    down_weight,
    out_weight,
    scan_input,
    delta_raw,
    mixer_gate_branch,
    state_input,
    state_output,
    log_rates,
    skip_gain,
    block_states,
):
    packed = pl.pallas_call(
        pack_kernel,
        out_shape=shape((8, 2, CAP, 256), BF16),
        in_specs=[VMEM] * 3,
        out_specs=VMEM,
        name="pack_rows",
    )(expert_ids, moe_input, out_grad)
    big = shape((TT * ROWS, 128))
    wide = shape((TT * 8, 128))
    rows, *saved, rate, decay, skip = pl.pallas_call(
        dispatch_kernel,
        out_shape=(shape((8, 16, 2, CAP, 256), BF16), big, big, big, big, wide, wide, wide,
                   shape((ROWS, 128)), shape((ROWS, 128)), shape((8, 128))),
        in_specs=[ANY] + [VMEM] * 7,
        out_specs=(ANY,) * 8 + (VMEM,) * 3,
        scratch_shapes=[pltpu.VMEM(big.shape, F32)] * 4 + [pltpu.VMEM(wide.shape, F32)] * 3
        + sems(24) + [pltpu.SemaphoreType.DMA, pltpu.SemaphoreType.DMA((7,))],
        compiler_params=talk(1),
        name="dispatch_and_scan",
    )(packed, scan_input, delta_raw, state_input, state_output, log_rates, block_states, skip_gain.reshape(1, 512))
    parts, probes = pl.pallas_call(
        expert_kernel,
        grid=(8,),
        out_shape=(shape((8, 16, CAP, 256), BF16), shape((8, 384))),
        in_specs=[
            pl.BlockSpec((8, 4, 2, CAP, 256), lambda i: (0, jnp.minimum(i, 3), 0, 0, 0)),
            pl.BlockSpec((1, 1024, 512), lambda i: (0, lax.rem(i, 4), 0)),
            pl.BlockSpec((1, 1024, 512), lambda i: (0, lax.rem(i, 4), 0)),
            pl.BlockSpec((1, 512, 1024), lambda i: (0, 0, jnp.minimum(i, 3))),
        ],
        out_specs=(
            pl.BlockSpec((8, 4, CAP, 256), lambda i: (0, jnp.maximum(i - 4, 0), 0, 0)),
            pl.BlockSpec((8, 384), lambda i: (0, 0)),
        ),
        scratch_shapes=[pltpu.VMEM((384, 512), F32)] * 3 + [pltpu.VMEM((384, 512), BF16)] * 2,
        name="experts",
    )(rows, gate_weight, up_weight, down_weight)
    returned, told = pl.pallas_call(
        combine_kernel,
        out_shape=(shape((16, CAP, 256), BF16), shape((16, 8, 128))),
        in_specs=[VMEM] * 2,
        out_specs=(VMEM,) * 2,
        scratch_shapes=[
            pltpu.VMEM((4, 16, CAP, 256), BF16),
            pltpu.VMEM((4, 16, CAP, 256), BF16),
            pltpu.VMEM((8, 8, CAP, 256), BF16),
            pltpu.VMEM((16, CAP, 256), BF16),
            pltpu.VMEM((7, 8, 384), F32),
            pltpu.VMEM((8, 128), F32),
        ] + sems(47) + [pltpu.SemaphoreType.DMA((2,))],
        compiler_params=talk(2),
        name="combine",
    )(parts, probes)
    resid_grad, probs_grad, inner_parts = pl.pallas_call(
        resid_kernel,
        grid=(4,),
        out_shape=(shape((TT, 256), BF16), shape((TT, 2)), shape((4, 4, TT, 512), BF16)),
        in_specs=[
            pl.BlockSpec((TT, 2), lambda i: (0, 0)),
            pl.BlockSpec((TT, 2), lambda i: (0, 0)),
            pl.BlockSpec((16, CAP, 256), lambda i: (0, 0, 0)),
            pl.BlockSpec((16, 8, 128), lambda i: (0, 0, 0)),
            pl.BlockSpec((TT, 256), lambda i: (0, 0)),
            pl.BlockSpec((2048, 256), lambda i: (i, 0)),
        ],
        out_specs=(
            pl.BlockSpec((TT, 256), lambda i: (0, 0)),
            pl.BlockSpec((TT, 2), lambda i: (0, 0)),
            pl.BlockSpec((1, 4, TT, 512), lambda i: (i, 0, 0, 0)),
        ),
        scratch_shapes=[pltpu.VMEM((TT, 256), BF16)],
        name="resid_and_inner",
    )(expert_ids, expert_route_weights, returned, told, out_grad, out_weight)
    gate_grad, input_grad, delta_grad, rates_grad, skip_grad = pl.pallas_call(
        tail_kernel,
        out_shape=(shape((512, 128), BF16),) * 3 + (shape((16, 512)), shape((1, 512))),
        in_specs=[ANY] * 8 + [VMEM] * 5,
        out_specs=(VMEM,) * 5,
        scratch_shapes=[pltpu.VMEM((4, 4, TT, 512), BF16)] + [pltpu.VMEM((8, 2, 64, 512), BF16)] * 2
        + [pltpu.VMEM((8, 32, 512), F32)] * 2 + [pltpu.VMEM((4, 64, 512), F32)] * 2 + [pltpu.VMEM((TT, 512), F32)]
        + [pltpu.VMEM(big.shape, F32)] * 4 + [pltpu.VMEM(wide.shape, F32)] * 6
        + [pltpu.VMEM((ROWS, 128), F32)] + [pltpu.VMEM((7, ROWS, 128), F32)] * 2
        + [pltpu.VMEM((72, 128), F32)] * 3 + [pltpu.VMEM((3, 72, 128), F32)]
        + sems(42) + [pltpu.SemaphoreType.DMA((8,))],
        compiler_params=talk(3),
        name="adjoint_tail",
    )(inner_parts, saved[0], saved[1], saved[2], saved[3], saved[4], saved[5], saved[6],
      mixer_gate_branch, delta_raw, rate, decay, skip)
    results = (gate_grad, input_grad, delta_grad, rates_grad, skip_grad)
    gate_grad, input_grad, delta_grad, rates_grad, skip_grad = pl.pallas_call(
        finish_kernel,
        out_shape=tuple(shape(r.shape, r.dtype) for r in results),
        in_specs=[VMEM] * 5,
        out_specs=(VMEM,) * 5,
        name="finish",
    )(*results)
    skip_grad = skip_grad.reshape(512)
    return (resid_grad, probs_grad, input_grad, delta_grad, gate_grad, rates_grad, skip_grad)


def solution(mesh):
    in_specs = (
        P("seq", "exp"),
        P("seq", "exp"),
        P("seq", None),
        P("seq", None),
        P("exp", None, "seq"),
        P("exp", None, "seq"),
        P("exp", "seq", None),
        P(None, "exp"),
        P("exp", "seq"),
        P("exp", "seq"),
        P("exp", "seq"),
        P(None, "seq"),
        P(None, "seq"),
        P(None, "exp"),
        P("exp"),
        P("seq", None, "exp"),
    )
    out_specs = (
        P("seq", "exp"),
        P("seq", None),
        P("exp", "seq"),
        P("exp", "seq"),
        P("exp", "seq"),
        P(None, "exp"),
        P("exp"),
    )
    return jax.shard_map(local, mesh=mesh, in_specs=in_specs, out_specs=out_specs, check_vma=False)
```

```python
import jax
import jax.numpy as jnp
from jax import lax
from jax.experimental import pallas as pl
from jax.experimental.pallas import tpu as pltpu
from jax.sharding import PartitionSpec as P

N_SEQ = 8
F32 = jnp.float32
BF16 = jnp.bfloat16
VMEM = pl.BlockSpec(memory_space=pltpu.VMEM)
SMEM = pl.BlockSpec(memory_space=pltpu.SMEM)


def shape(dims, kind=jnp.float32):
    return jax.ShapeDtypeStruct(dims, kind)


LOG2E = 1.4426950408889634
GR = 4
TT = 128
ROWS = 64


def softplus(v):
    return jnp.maximum(v, 0.0) + jnp.log1p(jnp.exp(-jnp.abs(v)))


def sigmoid(v):
    return 1.0 / (1.0 + jnp.exp(-v))


def spread(ref, g, val):
    ref[pl.ds(g, TT, stride=8), :] = val
    ref[pl.ds(GR + g, TT, stride=8), :] = val


def column(rep, t):
    return jnp.take_along_axis(rep, jnp.full((8, 128), t, jnp.int32), axis=1)


def grouped(ref, j):
    return jnp.concatenate(
        [ref[2 * j + p:2 * j + p + 1, g * 128:(g + 1) * 128] for p in range(2) for g in range(GR)], axis=0)


def doubled(ref, j):
    return jnp.concatenate(
        [jnp.broadcast_to(ref[2 * j + p:2 * j + p + 1, :], (GR, 128)) for p in range(2)], axis=0)


def octet(j):
    return slice(8 * j, 8 * j + 8)


def at_token(t):
    return pl.ds(pl.multiple_of(t * 8, 8), 8)


def at_state(t, j):
    return pl.ds(pl.multiple_of(t * ROWS, ROWS) + 8 * j, 8)


class Forward:
    def __init__(self, u, d, b, c, lr, st, sk, rate, decay, skip, a, ear, bb, cb, dt, us, so):
        self.__dict__.update(locals())

    def open(self):
        for g in range(GR):
            rows = pl.ds(g * 128, 128)
            spread(self.dt, g, softplus(self.d[rows, :].astype(F32).T))
            spread(self.us, g, self.u[rows, :].astype(F32).T)
        for j in range(8):
            self.rate[octet(j), :] = jnp.exp(grouped(self.lr, j))
        self.skip[...] = jnp.concatenate(
            [self.sk[0:1, g * 128:(g + 1) * 128] for p in range(2) for g in range(GR)], axis=0)
        one = jnp.ones((8, 128), F32)
        return tuple(grouped(self.st.at[0], j) for j in range(8)) + (one,) * 8

    def run(self, first, last, carry):
        rate2 = [-LOG2E * self.rate[octet(j), :] for j in range(8)]
        b_rep = [doubled(self.b, j) for j in range(8)]
        c_rep = [doubled(self.c, j) for j in range(8)]
        skip = self.skip[...]

        def step(t, carry):
            here = at_token(t)
            dt = self.dt[here, :]
            u = self.us[here, :]
            du = dt * u
            acc = jnp.zeros((8, 128), F32)
            states, products = [], []
            for j in range(8):
                spot = at_state(t, j)
                b = column(b_rep[j], t)
                c = column(c_rep[j], t)
                a = jnp.exp2(dt * rate2[j])
                state = a * carry[j] + du * b
                self.ear[spot, :] = carry[j]
                self.a[spot, :] = a
                self.bb[spot, :] = b
                self.cb[spot, :] = c
                acc = acc + c * state
                states.append(state)
                products.append(carry[8 + j] * a)
            self.so[here, :] = acc + pltpu.roll(acc, 4, 0) + skip * u
            return tuple(states + products)

        return lax.fori_loop(first, last, step, carry)

    def close(self, carry):
        for j in range(8):
            self.decay[octet(j), :] = carry[8 + j]


MESH = pl.DeviceIdType.MESH
ANY = pl.BlockSpec(memory_space=pl.ANY)
CAP = 48


def places():
    q = lax.axis_index("seq")
    e = lax.axis_index("exp")
    return q, e


def knock(peers):
    for peer in peers:
        pl.semaphore_signal(pltpu.get_barrier_semaphore(), inc=1, device_id=peer, device_id_type=MESH)


def greeted(peers):
    pl.semaphore_wait(pltpu.get_barrier_semaphore(), len(peers))


class Copies:
    def __init__(self, send, recv):
        self.send, self.recv, self.all, self.next = send, recv, [], 0

    def make(self, src, dst, peer):
        n = self.next
        self.next = n + 1
        return pltpu.make_async_remote_copy(
            src_ref=src, dst_ref=dst, send_sem=self.send.at[n], recv_sem=self.recv.at[n],
            device_id=peer, device_id_type=MESH,
        )

    def start(self, src, dst, peer):
        copy = self.make(src, dst, peer)
        copy.start()
        self.all.append(copy)
        return copy

    def finish(self):
        for copy in self.all:
            copy.wait_send()


def seq_at(y, c):
    return lax.rem(y + 4, 4) * 2 + c


def added(out, first, *others):
    total = first.astype(F32)
    for other in others:
        total = total + other.astype(F32)
    return total.astype(out)


class Ring:
    def __init__(self, cp, place, up, down, block, land):
        self.cp, self.p, self.up, self.down, self.block, self.land = cp, place, up, down, block, land

    def at(self, step, half, own=1):
        return self.block(lax.rem(self.p + step + 4, 4), half)[own]

    def far(self):
        cp, land = self.cp, self.land
        self.u2 = cp.start(self.at(2, 0, 0), land.at[0], self.up)
        self.d2 = cp.start(self.at(2, 1, 0), land.at[1], self.down)

    def near(self):
        cp, land = self.cp, self.land
        self.uh = cp.start(self.at(1, 1, 0), land.at[2], self.up)
        self.dl = cp.start(self.at(-1, 0, 0), land.at[3], self.down)

    def second(self, add):
        cp, land = self.cp, self.land
        self.u2.wait_recv()
        add(land.at[6], self.at(1, 0), land.at[0])
        self.ul = cp.start(land.at[6], land.at[4], self.up)
        self.d2.wait_recv()
        add(land.at[7], self.at(-1, 1), land.at[1])
        self.dh = cp.start(land.at[7], land.at[5], self.down)

    def last(self, add, outs):
        land = self.land
        self.dl.wait_recv()
        self.ul.wait_recv()
        add(outs[0], self.at(0, 0), land.at[4], land.at[3])
        self.uh.wait_recv()
        self.dh.wait_recv()
        add(outs[1], self.at(0, 1), land.at[2], land.at[5])


def add_rows(count):
    def add(out, *refs):
        @pl.loop(0, count)
        def _(n):
            out[n] = added(out.dtype, *[ref[n] for ref in refs])
    return add


def sems(count):
    return [pltpu.SemaphoreType.DMA((count,))] * 2


def talk(number, limit=None):
    return pltpu.CompilerParams(collective_id=number, has_side_effects=True, vmem_limit_bytes=limit)


NT = (((1,), (1,)), ((), ()))


def slots_of(ids):
    expert = lax.broadcasted_iota(jnp.int32, (8, TT), 0)
    hits = [(ids[k:k + 1, :] == expert).astype(F32) for k in range(2)]
    first = lax.broadcasted_iota(jnp.int32, (TT, TT), 0)
    second = lax.broadcasted_iota(jnp.int32, (TT, TT), 1)
    ahead = (first < second).astype(F32).astype(BF16)
    before = jnp.dot((hits[0] + hits[1]).astype(BF16), ahead, preferred_element_type=F32)
    return [jnp.sum(hit * before, axis=0, keepdims=True).astype(jnp.int32) for hit in hits]


def pack(ids_ref, x_ref, g_ref, s_ref):
    ids = ids_ref[...]
    slots = slots_of(ids)
    row = lax.broadcasted_iota(jnp.int32, (8 * CAP, TT), 0)
    hit = jnp.zeros((8 * CAP, TT), F32)
    for k in range(2):
        hit = hit + (ids[k:k + 1, :] * CAP + slots[k] == row).astype(F32)
    hot = hit.astype(BF16)
    for a, ref in enumerate((x_ref, g_ref)):
        rows = jnp.dot(hot, ref[...], preferred_element_type=F32).astype(BF16)
        for n in range(8):
            s_ref[n, a] = rows[n * CAP:(n + 1) * CAP, :]


class Arrival:
    def __init__(self, cp, arr, s, r, near):
        self.cp, self.arr, self.s, self.r, self.near = cp, arr, s, r, near
        q, e = places()
        self.q, self.e, self.h = q, e, lax.rem(e, 2)
        y, c = q // 2, lax.rem(q, 2)
        self.qu, self.qd, self.q2 = seq_at(y + 1, c), seq_at(y - 1, c), seq_at(y + 2, c)
        self.up, self.down, self.core = (self.qu, e), (self.qd, e), (y * 2 + 1 - c, e)
        self.pair = (q, e + 1 - 2 * self.h)
        self.across, self.cores = [], []

    def exchange(self):
        s, r, q, e, arr = self.s, self.r, self.q, self.e, self.arr
        x, z = e // 4, lax.rem(e, 4)

        def at(dx, dz):
            return lax.rem(x + dx, 4) * 4 + lax.rem(z + dz, 4)

        self.own = pltpu.make_async_copy(s.at[e // 2, arr], r.at[q, arr, x, z], self.near)
        self.own.start()
        self.parts = [
            self.cp.start(s.at[at(dx, dz) // 2, arr], r.at[q, arr, x, z], (q, at(dx, dz)))
            for dx in (2, 1, 3, 0) for dz in (2, 1, 3, 0) if (dx, dz) != (0, 0)]
    def move(self, shard, at, size, peer):
        ref = self.r.at[shard, self.arr, pl.ds(at, size)]
        return self.cp.start(ref, ref, peer)

    def pass_on(self, shard, at, size):
        self.cores.append(self.move(shard, at, size, self.core))

    def start(self):
        self.own.wait()
        for part in self.parts:
            part.wait_recv()
        self.a = self.move(self.q, self.h, 3, self.up)
        self.b = self.move(self.q, self.h, 3, self.down)
        self.pass_on(self.q, 0, 4)

    def middle(self):
        h = self.h
        self.a.wait_recv()
        self.f = self.move(self.qd, 2 * h, 1, self.up)
        self.across.append((self.qd, 3 - 3 * h, self.move(self.qd, 3 * h, 1, self.pair)))
        self.pass_on(self.qd, h, 3)
        self.b.wait_recv()
        self.g = self.move(self.qu, 2 * h + 1, 1, self.down)
        self.across.append((self.qu, 3 - 3 * h, self.move(self.qu, 3 * h, 1, self.pair)))
        self.pass_on(self.qu, h, 3)

    def late(self):
        h, q2 = self.h, self.q2
        self.f.wait_recv()
        self.across.append((q2, 2 - 2 * h, self.move(q2, 2 * h, 1, self.pair)))
        self.pass_on(q2, 2 * h, 1)
        self.g.wait_recv()
        self.across.append((q2, 3 - 2 * h, self.move(q2, 2 * h + 1, 1, self.pair)))
        self.pass_on(q2, 2 * h + 1, 1)
        for shard, at, copy in self.across:
            copy.wait_recv()
            self.pass_on(shard, at, 1)

    def end(self):
        for copy in self.cores:
            copy.wait_recv()


def resid_of(ids_ref, w_ref, t_ref, tp_ref, g_ref, probs_ref):
    ids = ids_ref[...]
    slots = slots_of(ids)
    weights = w_ref[...]
    table = jnp.concatenate(
        [ids[k:k + 1, :].astype(F32) for k in range(2)] + [slots[k].astype(F32) for k in range(2)]
        + [weights[k:k + 1, :] for k in range(2)] + [jnp.zeros((2, TT), F32)], axis=0).T
    lane = lax.broadcasted_iota(jnp.int32, (TT, 8 * CAP), 1)
    near = lax.broadcasted_iota(jnp.int32, (TT, 128), 1)
    total = g_ref[...].astype(F32)
    even = jnp.concatenate([t_ref[2 * n] for n in range(8)], axis=0)
    odd = jnp.concatenate([t_ref[2 * n + 1] for n in range(8)], axis=0)
    probs = []
    for k in range(2):
        name = table[:, k:k + 1].astype(jnp.int32)
        slot = table[:, 2 + k:3 + k].astype(jnp.int32)
        hot = (name * CAP + slot == lane).astype(F32).astype(BF16)
        route = jnp.dot(hot, even, preferred_element_type=F32) + jnp.dot(hot, odd, preferred_element_type=F32)
        total = total + table[:, 4 + k:5 + k] * route
        acc = jnp.zeros((TT, 128), F32)
        for n in range(8):
            row = tp_ref[2 * n, 0:1, :] + tp_ref[2 * n + 1, 0:1, :]
            acc = acc + jnp.where((name == n) & (slot == near), row, 0.0)
        probs.append(jnp.sum(acc, axis=1, keepdims=True))
    probs_ref[...] = jnp.concatenate(probs + [jnp.zeros((TT, 6), F32)], axis=1).T[:2, :]
    return total.astype(BF16)


def layer_kernel(ids_ref, w_ref, x_ref, g_ref, u, d, b_ref, c_ref, lr, st, sk, z_ref, wg_h, wu_h, wd_h, ow_h,
                 res_ref, probs_ref, gate_ref, input_ref, delta_ref, rates_ref, skipped_ref,
                 s_ref, r_ref, wg, wu, wd, gate, up, hid, dg, du, parts, pair, sums, land, final, probe, probes, mine,
                 t_ref, tp_ref, rate_ref, decay_ref, skip_ref, a, ear, bb, cb, dt, us, so,
                 ow, sent, lx, lz, kx, kz, jx, jz, inner, ys, s1s, dls,
                 term, terms, decays, part, other, both, three, send, recv, near):
    q, e = places()
    y, c = q // 2, lax.rem(q, 2)
    x, z = e // 4, lax.rem(e, 4)
    far = [(q, lax.rem(e + k, 16)) for k in range(1, 16)]
    rows = [(lax.rem(q + k, 8), e) for k in range(1, 8)]
    core = (y * 2 + 1 - c, e)
    xu, xd = (q, lax.rem(x + 1, 4) * 4 + z), (q, lax.rem(x + 3, 4) * 4 + z)
    zu, zd = (q, x * 4 + lax.rem(z + 1, 4)), (q, x * 4 + lax.rem(z + 3, 4))
    weights = [pltpu.make_async_copy(src.at[0], dst, near.at[n]) for n, (src, dst) in enumerate(
        ((wg_h, wg), (wu_h, wu), (wd_h, wd)))]
    late_load = pltpu.make_async_copy(ow_h, ow, near.at[5])
    terms[...] = jnp.zeros_like(terms)
    decays[...] = jnp.zeros_like(decays)
    knock(far + rows)
    pack(ids_ref, x_ref, g_ref, s_ref)
    for weight in weights:
        weight.start()
    late_load.start()
    greeted(far + rows)
    cp = Copies(send, recv)
    xs, gs = Arrival(cp, 0, s_ref, r_ref, near.at[3]), Arrival(cp, 1, s_ref, r_ref, near.at[4])
    xs.exchange()
    gs.exchange()
    scan = Forward(u, d, b_ref, c_ref, lr, st, sk, rate_ref, decay_ref, skip_ref, a, ear, bb, cb, dt, us, so)
    carry = scan.run(0, 40, scan.open())
    xs.start()
    scan.close(scan.run(40, TT, carry))
    xs.middle()
    gs.start()
    xs.late()
    gs.middle()
    xs.end()
    for weight in weights:
        weight.wait()

    def rows_of(arr, k):
        return jnp.concatenate([r_ref[:, arr, k, n].reshape(384, 256) for n in range(4)], axis=1)

    gate[...] = jnp.zeros_like(gate)
    up[...] = jnp.zeros_like(up)
    hid[...] = jnp.zeros_like(hid)

    @pl.loop(0, 4)
    def _(k):
        deep = pl.ds(pl.multiple_of(k * 1024, 1024), 1024)
        lhs = rows_of(0, k)
        gate[...] += jnp.dot(lhs, wg[deep, :], preferred_element_type=F32)
        up[...] += jnp.dot(lhs, wu[deep, :], preferred_element_type=F32)

    gs.late()
    gs.end()

    @pl.loop(0, 4)
    def _(k):
        deep = pl.ds(pl.multiple_of(k * 1024, 1024), 1024)
        hid[...] += lax.dot_general(rows_of(1, k), wd[:, deep], NT, preferred_element_type=F32)

    v, w, h = gate[...], up[...], hid[...]
    sig = sigmoid(v)
    dg[...] = (h * w * sig * (1.0 + v * (1.0 - sig))).astype(BF16)
    gu = h * (v * sig)
    du[...] = gu.astype(BF16)
    order = [2, 1, 3, 0]
    four = [pl.multiple_of(lax.rem(x + n, 4) * 4, 4) for n in order]
    halves, rings, shares = [], [], []

    def multiply(i):
        deep = pl.ds(pl.multiple_of(four[i] * 256, 1024), 1024)
        part = lax.dot_general(dg[...], wg[deep, :], NT, preferred_element_type=F32)
        part = part + lax.dot_general(du[...], wu[deep, :], NT, preferred_element_type=F32)
        for n in range(4):
            parts[:, :, four[i] + n] = part[:, n * 256:(n + 1) * 256].reshape(4, 2, CAP, 256).astype(BF16)
        here = pl.ds(four[i], 4)
        halves.append(cp.start(parts.at[:, 1 - c, here], pair.at[:, here], core))

    def join(i):
        halves[i].wait_recv()

        @pl.loop(0, 16)
        def _(n):
            j, m = n // 4, four[i] + lax.rem(n, 4)
            sums[j, m] = added(BF16, parts[j, c, m], pair[j, m])

        ring = Ring(cp, y, (seq_at(y + 1, c), e), (seq_at(y - 1, c), e),
                    lambda d, half: (sums.at[d, pl.ds(four[i] + 2 * half, 2)],) * 2, land.at[i])
        ring.far()
        ring.near()
        rings.append(ring)

    two = add_rows(2)

    def leave(i):
        rings[i].last(two, (final.at[pl.ds(four[i], 2)], final.at[pl.ds(four[i] + 2, 2)]))
        for m in range(4):
            to = four[i] + lax.rem(z + m, 4)
            if order[i] == 0 and m == 0:
                own = pltpu.make_async_copy(final.at[to], t_ref.at[e], near.at[6])
                own.start()
                leave.own = own
            else:
                shares.append(cp.start(final.at[to], t_ref.at[e], (q, to)))

    multiply(0)
    held = gu * w
    held = held[:, :128] + held[:, 128:256] + held[:, 256:384] + held[:, 384:]
    probe[...] = jnp.broadcast_to(jnp.sum(held.T, axis=0, keepdims=True), (8, 384))
    tells = [cp.start(probe, probes.at[k], rows[k]) for k in range(7)]
    multiply(1)
    join(0)
    multiply(2)
    join(1)
    rings[0].second(two)
    multiply(3)
    join(2)
    rings[1].second(two)
    leave(0)
    join(3)
    rings[2].second(two)
    leave(1)
    for tell in tells:
        tell.wait_recv()
    total = probe[...]
    for k in range(7):
        total = total + probes[k]
    mine[...] = pltpu.roll(total, lax.rem(8 - q, 8) * CAP, 1)[:, :128]
    rings[3].second(two)
    own_probe = pltpu.make_async_copy(mine, tp_ref.at[e], near.at[7])
    own_probe.start()
    shares += [cp.start(mine, tp_ref.at[e], peer) for peer in far]
    leave(2)
    leave(3)
    own_probe.wait()
    leave.own.wait()
    for share in shares:
        share.wait_recv()

    def earlier_shards(src, land):
        copies = []
        for k in range(1, 8):
            copy = cp.make(src, land.at[k - 1], (lax.rem(q + 8 - k, 8), e))

            @pl.when(q >= k)
            def _(copy=copy):
                copy.start()
            copies.append(copy)

        def arrive():
            for k in range(1, 8):
                @pl.when(q + k < 8)
                def _(k=k):
                    copies[k - 1].wait_recv()

        def leave():
            for k in range(1, 8):
                @pl.when(q >= k)
                def _(k=k):
                    copies[k - 1].wait_send()
        return arrive, leave

    late_load.wait()
    res_ref[...] = resid_of(ids_ref, w_ref, t_ref, tp_ref, g_ref, probs_ref)
    resid = res_ref[...]

    def inner_part(d):
        for n in range(4):
            rows = pl.ds(pl.multiple_of(d * 2048, 2048) + 512 * n, 512)
            sent[d, n] = lax.dot_general(ow[rows, :], resid, NT, preferred_element_type=F32).astype(BF16)

    def x_block(i):
        def block(d, half):
            return (sent.at[d, pl.ds(2 * half, 2), pl.ds(128 * i, 128)],) * 2
        return block

    def z_block(i):
        def block(d, half):
            return (sent.at[pl.ds(2 * half, 2), d, pl.ds(256 + 128 * i, 128)],) * 2
        return block

    def then(ref):
        def block(d, half):
            return (ref.at[d, pl.ds(64 * half, 64)],) * 2
        return block

    def one(out, *refs):
        out[...] = added(out.dtype, *[ref[...] for ref in refs])

    rx = [Ring(cp, x, xu, xd, x_block(i), lx.at[i]) for i in range(2)]
    rz = [Ring(cp, z, zu, zd, z_block(i), lz.at[i]) for i in range(2)]
    sx = [Ring(cp, z, zu, zd, then(jx.at[i]), kx.at[i]) for i in range(2)]
    sz = [Ring(cp, x, xu, xd, then(jz.at[i]), kz.at[i]) for i in range(2)]
    inner_part(lax.rem(x + 2, 4))
    for ring in rx:
        ring.far()
    inner_part(lax.rem(x + 1, 4))
    inner_part(lax.rem(x + 3, 4))
    inner_part(x)
    for ring in rz:
        ring.far()
    for ring in rx + rz:
        ring.near()
    decays_in, decays_out = earlier_shards(decay_ref, decays)
    for i in range(2):
        rx[i].second(two)
        rz[i].second(two)
    for i in range(2):
        rx[i].last(two, (jx.at[i, pl.ds(0, 2)], jx.at[i, pl.ds(2, 2)]))
        sx[i].far()
        rz[i].last(two, (jz.at[i, pl.ds(0, 2)], jz.at[i, pl.ds(2, 2)]))
        sz[i].far()
        sx[i].near()
        sz[i].near()
    for i in range(2):
        sx[i].second(one)
        sz[i].second(one)
    for i in range(2):
        sx[i].last(one, (inner.at[pl.ds(128 * i, 64)], inner.at[pl.ds(128 * i + 64, 64)]))
        sz[i].last(one, (inner.at[pl.ds(256 + 128 * i, 64)], inner.at[pl.ds(320 + 128 * i, 64)]))

    for g in range(GR):
        rows = pl.ds(g * 128, 128)
        act = z_ref[rows, :].astype(F32)
        spread(ys, g, (inner[rows, :] * act * sigmoid(act)).T)

    zero = jnp.zeros((8, 128), F32)

    def summary(i, carry):
        t = TT - 1 - i
        grad = ys[at_token(t), :]
        return tuple(a[at_state(t, j), :] * (cb[at_state(t, j), :] * grad + carry[j]) for j in range(8))

    last = lax.fori_loop(0, TT, summary, (zero,) * 8, unroll=4)
    for j in range(8):
        term[octet(j), :] = last[j]
    terms_in, terms_out = earlier_shards(term, terms)

    for g in range(GR):
        rows = pl.ds(g * 128, 128)
        act = z_ref[rows, :].astype(F32)
        sig = sigmoid(act)
        gated = inner[rows, :] * so[pl.ds(g, TT, stride=8), :].T * sig * (1.0 + act * (1.0 - sig))
        gate_ref[rows, :] = gated.astype(BF16)

    decays_in()
    terms_in()
    rate = [rate_ref[octet(j), :] for j in range(8)]
    start = []
    for j in range(8):
        inc = zero
        for k in range(7, 0, -1):
            inc = terms[k - 1, octet(j), :] + decays[k - 1, octet(j), :] * inc
        start.append(inc)

    def step(i, carry):
        vs, sums, sk = carry
        t = TT - 1 - i
        here = at_token(t)
        grad = ys[here, :]
        size = dt[here, :]
        s1, dl = zero, zero
        nv, ns = [], []
        for j in range(8):
            spot = at_state(t, j)
            adj = cb[spot, :] * grad + vs[j]
            v = a[spot, :] * adj
            w = v * ear[spot, :]
            s1 = s1 + adj * bb[spot, :]
            dl = dl + rate[j] * w
            ns.append(sums[j] + size * w)
            nv.append(v)
        s1s[here, :] = s1 + pltpu.roll(s1, 4, 0)
        dls[here, :] = dl + pltpu.roll(dl, 4, 0)
        return tuple(nv), tuple(ns), sk + grad * us[here, :]

    vs, sums, sk = lax.fori_loop(0, TT, step, (tuple(start), (zero,) * 8, zero), unroll=2)
    for j in range(8):
        part[octet(j), :] = -rate[j] * sums[j]
    part[64:72, :] = sk
    swap = cp.start(part, other, (y * 2 + 1 - c, e))

    for g in range(GR):
        rows = pl.ds(g * 128, 128)
        mine = pl.ds(g, TT, stride=8)
        s1 = s1s[mine, :]
        inp = s1 * dt[mine, :] + skip_ref[g:g + 1, :] * ys[mine, :]
        input_ref[rows, :] = inp.T.astype(BF16)

    swap.wait_recv()
    both[...] = part[...] + other[...]
    shares = [cp.start(both, three.at[k - 1], (seq_at(y + k, c), e)) for k in range(1, 4)]

    for g in range(GR):
        rows = pl.ds(g * 128, 128)
        mine = pl.ds(g, TT, stride=8)
        step_grad = us[mine, :] * s1s[mine, :] - dls[mine, :]
        delta_ref[rows, :] = (step_grad.T * sigmoid(d[rows, :].astype(F32))).astype(BF16)

    for share in shares:
        share.wait_recv()
    both2 = both[...] + three[0] + three[1] + three[2]
    for j in range(8):
        for p in range(2):
            for g in range(GR):
                row = 8 * j + GR * p + g
                rates_ref[2 * j + p:2 * j + p + 1, g * 128:(g + 1) * 128] = both2[row:row + 1, :]
    for g in range(GR):
        skipped_ref[0:1, g * 128:(g + 1) * 128] = both2[64 + g:65 + g, :]
    decays_out()
    terms_out()
    cp.finish()


def finish_kernel(*refs):
    for src, dst in zip(refs[:7], refs[7:]):
        dst[...] = src[...]


def local(
    moe_input,
    out_grad,
    expert_ids,
    expert_route_weights,
    gate_weight,
    up_weight,
    down_weight,
    out_weight,
    scan_input,
    delta_raw,
    mixer_gate_branch,
    state_input,
    state_output,
    log_rates,
    skip_gain,
    block_states,
):
    block = pltpu.VMEM((4, 16, CAP, 256), BF16)
    results = pl.pallas_call(
        layer_kernel,
        out_shape=(shape((TT, 256), BF16), shape((2, TT))) + (shape((512, 128), BF16),) * 3
        + (shape((16, 512)), shape((1, 512))),
        in_specs=[VMEM] * 12 + [ANY] * 4,
        out_specs=(VMEM,) * 7,
        scratch_shapes=[
            pltpu.VMEM((8, 2, CAP, 256), BF16),
            pltpu.VMEM((8, 2, 4, 4, CAP, 256), BF16),
            pltpu.VMEM((4096, 512), BF16),
            pltpu.VMEM((4096, 512), BF16),
            pltpu.VMEM((512, 4096), BF16),
        ] + [pltpu.VMEM((384, 512), F32)] * 3 + [pltpu.VMEM((384, 512), BF16)] * 2
        + [pltpu.VMEM((4, 2, 16, CAP, 256), BF16), block, block, pltpu.VMEM((4, 8, 2, CAP, 256), BF16),
           pltpu.VMEM((16, CAP, 256), BF16), pltpu.VMEM((8, 384), F32), pltpu.VMEM((7, 8, 384), F32),
           pltpu.VMEM((8, 128), F32), pltpu.VMEM((16, CAP, 256), BF16), pltpu.VMEM((16, 8, 128), F32)]
        + [pltpu.VMEM((ROWS, 128), F32)] * 2 + [pltpu.VMEM((8, 128), F32)]
        + [pltpu.VMEM((TT * ROWS, 128), F32)] * 4 + [pltpu.VMEM((TT * 8, 128), F32)] * 3
        + [pltpu.VMEM((8192, 256), BF16), pltpu.VMEM((4, 4, 512, TT), BF16)]
        + [pltpu.VMEM((2, 8, 2, 128, TT), BF16)] * 2 + [pltpu.VMEM((2, 8, 64, TT), F32)] * 2
        + [pltpu.VMEM((2, 4, 128, TT), F32)] * 2 + [pltpu.VMEM((512, TT), F32)]
        + [pltpu.VMEM((TT * 8, 128), F32)] * 3
        + [pltpu.VMEM((ROWS, 128), F32)] + [pltpu.VMEM((7, ROWS, 128), F32)] * 2
        + [pltpu.VMEM((72, 128), F32)] * 3 + [pltpu.VMEM((3, 72, 128), F32)]
        + sems(195) + [pltpu.SemaphoreType.DMA((8,))],
        compiler_params=talk(1, 67043328),
        name="layer_backward",
    )(expert_ids.T, expert_route_weights.T, moe_input, out_grad, scan_input, delta_raw, state_input, state_output,
      log_rates, block_states, skip_gain.reshape(1, 512), mixer_gate_branch, gate_weight, up_weight, down_weight, out_weight)
    resid_grad, probs_grad, gate_grad, input_grad, delta_grad, rates_grad, skip_grad = pl.pallas_call(
        finish_kernel,
        out_shape=tuple(shape(r.shape, r.dtype) for r in results),
        in_specs=[VMEM] * 7,
        out_specs=(VMEM,) * 7,
        name="finish",
    )(*results)
    skip_grad = skip_grad.reshape(512)
    return (resid_grad, probs_grad.T, input_grad, delta_grad, gate_grad, rates_grad, skip_grad)


def solution(mesh):
    in_specs = (
        P("seq", "exp"),
        P("seq", "exp"),
        P("seq", None),
        P("seq", None),
        P("exp", None, "seq"),
        P("exp", None, "seq"),
        P("exp", "seq", None),
        P(None, "exp"),
        P("exp", "seq"),
        P("exp", "seq"),
        P("exp", "seq"),
        P(None, "seq"),
        P(None, "seq"),
        P(None, "exp"),
        P("exp"),
        P("seq", None, "exp"),
    )
    out_specs = (
        P("seq", "exp"),
        P("seq", None),
        P("exp", "seq"),
        P("exp", "seq"),
        P("exp", "seq"),
        P(None, "exp"),
        P("exp"),
    )
    return jax.shard_map(local, mesh=mesh, in_specs=in_specs, out_specs=out_specs, check_vma=False)
```

```python
import jax
import jax.numpy as jnp
from jax import lax
from jax.experimental import pallas as pl
from jax.experimental.pallas import tpu as pltpu
from jax.sharding import PartitionSpec as P

N_SEQ = 8
F32 = jnp.float32
BF16 = jnp.bfloat16
VMEM = pl.BlockSpec(memory_space=pltpu.VMEM)
SMEM = pl.BlockSpec(memory_space=pltpu.SMEM)


def shape(dims, kind=jnp.float32):
    return jax.ShapeDtypeStruct(dims, kind)


LOG2E = 1.4426950408889634
GR = 4
TT = 128
ROWS = 64


def softplus(v):
    return jnp.maximum(v, 0.0) + jnp.log1p(jnp.exp(-jnp.abs(v)))


def sigmoid(v):
    return 1.0 / (1.0 + jnp.exp(-v))


def spread(ref, g, val):
    ref[pl.ds(g, TT, stride=8), :] = val
    ref[pl.ds(GR + g, TT, stride=8), :] = val


def column(rep, t):
    return jnp.take_along_axis(rep, jnp.full((8, 128), t, jnp.int32), axis=1)


def grouped(ref, j):
    return jnp.concatenate(
        [ref[2 * j + p:2 * j + p + 1, g * 128:(g + 1) * 128] for p in range(2) for g in range(GR)], axis=0)


def doubled(ref, j):
    return jnp.concatenate(
        [jnp.broadcast_to(ref[2 * j + p:2 * j + p + 1, :], (GR, 128)) for p in range(2)], axis=0)


def octet(j):
    return slice(8 * j, 8 * j + 8)


def at_token(t):
    return pl.ds(pl.multiple_of(t * 8, 8), 8)


def at_state(t, j):
    return pl.ds(pl.multiple_of(t * ROWS, ROWS) + 8 * j, 8)


class Forward:
    def __init__(self, u, d, b, c, lr, st, sk, rate, decay, skip, a, ear, bb, cb, dt, us, so):
        self.__dict__.update(locals())

    def open(self):
        for g in range(GR):
            rows = pl.ds(g * 128, 128)
            spread(self.dt, g, softplus(self.d[rows, :].astype(F32).T))
            spread(self.us, g, self.u[rows, :].astype(F32).T)
        for j in range(8):
            self.rate[octet(j), :] = jnp.exp(grouped(self.lr, j))
        self.skip[...] = jnp.concatenate(
            [self.sk[0:1, g * 128:(g + 1) * 128] for p in range(2) for g in range(GR)], axis=0)
        one = jnp.ones((8, 128), F32)
        return tuple(grouped(self.st.at[0], j) for j in range(8)) + (one,) * 8

    def run(self, first, last, carry):
        rate2 = [-LOG2E * self.rate[octet(j), :] for j in range(8)]
        b_rep = [doubled(self.b, j) for j in range(8)]
        c_rep = [doubled(self.c, j) for j in range(8)]
        skip = self.skip[...]

        def step(t, carry):
            here = at_token(t)
            dt = self.dt[here, :]
            u = self.us[here, :]
            du = dt * u
            acc = jnp.zeros((8, 128), F32)
            states, products = [], []
            for j in range(8):
                spot = at_state(t, j)
                b = column(b_rep[j], t)
                c = column(c_rep[j], t)
                a = jnp.exp2(dt * rate2[j])
                state = a * carry[j] + du * b
                self.ear[spot, :] = carry[j]
                self.a[spot, :] = a
                self.bb[spot, :] = b
                self.cb[spot, :] = c
                acc = acc + c * state
                states.append(state)
                products.append(carry[8 + j] * a)
            self.so[here, :] = acc + pltpu.roll(acc, 4, 0) + skip * u
            return tuple(states + products)

        return lax.fori_loop(first, last, step, carry)

    def close(self, carry):
        for j in range(8):
            self.decay[octet(j), :] = carry[8 + j]


MESH = pl.DeviceIdType.MESH
ANY = pl.BlockSpec(memory_space=pl.ANY)
CAP = 48


def places():
    q = lax.axis_index("seq")
    e = lax.axis_index("exp")
    return q, e


def knock(peers):
    for peer in peers:
        pl.semaphore_signal(pltpu.get_barrier_semaphore(), inc=1, device_id=peer, device_id_type=MESH)


def greeted(peers):
    pl.semaphore_wait(pltpu.get_barrier_semaphore(), len(peers))


class Copies:
    def __init__(self, send, recv):
        self.send, self.recv, self.all, self.next = send, recv, [], 0

    def make(self, src, dst, peer):
        n = self.next
        self.next = n + 1
        return pltpu.make_async_remote_copy(
            src_ref=src, dst_ref=dst, send_sem=self.send.at[n], recv_sem=self.recv.at[n],
            device_id=peer, device_id_type=MESH,
        )

    def start(self, src, dst, peer):
        copy = self.make(src, dst, peer)
        copy.start()
        self.all.append(copy)
        return copy

    def finish(self):
        for copy in self.all:
            copy.wait_send()


def seq_at(y, c):
    return lax.rem(y + 4, 4) * 2 + c


def added(out, first, *others):
    total = first.astype(F32)
    for other in others:
        total = total + other.astype(F32)
    return total.astype(out)


class Ring:
    def __init__(self, cp, place, up, down, block, land):
        self.cp, self.p, self.up, self.down, self.block, self.land = cp, place, up, down, block, land

    def at(self, step, half, own=1):
        return self.block(lax.rem(self.p + step + 4, 4), half)[own]

    def far(self):
        cp, land = self.cp, self.land
        self.u2 = cp.start(self.at(2, 0, 0), land.at[0], self.up)
        self.d2 = cp.start(self.at(2, 1, 0), land.at[1], self.down)

    def near(self):
        cp, land = self.cp, self.land
        self.uh = cp.start(self.at(1, 1, 0), land.at[2], self.up)
        self.dl = cp.start(self.at(-1, 0, 0), land.at[3], self.down)

    def second(self, add):
        cp, land = self.cp, self.land
        self.u2.wait_recv()
        add(land.at[6], self.at(1, 0), land.at[0])
        self.ul = cp.start(land.at[6], land.at[4], self.up)
        self.d2.wait_recv()
        add(land.at[7], self.at(-1, 1), land.at[1])
        self.dh = cp.start(land.at[7], land.at[5], self.down)

    def last(self, add, outs):
        land = self.land
        self.dl.wait_recv()
        self.ul.wait_recv()
        add(outs[0], self.at(0, 0), land.at[4], land.at[3])
        self.uh.wait_recv()
        self.dh.wait_recv()
        add(outs[1], self.at(0, 1), land.at[2], land.at[5])


def add_rows(count):
    def add(out, *refs):
        @pl.loop(0, count)
        def _(n):
            out[n] = added(out.dtype, *[ref[n] for ref in refs])
    return add


def sems(count):
    return [pltpu.SemaphoreType.DMA((count,))] * 2


def talk(number, limit=None):
    return pltpu.CompilerParams(collective_id=number, has_side_effects=True, vmem_limit_bytes=limit)


NT = (((1,), (1,)), ((), ()))


def slots_of(ids):
    expert = lax.broadcasted_iota(jnp.int32, (8, TT), 0)
    hits = [(ids[k:k + 1, :] == expert).astype(F32) for k in range(2)]
    first = lax.broadcasted_iota(jnp.int32, (TT, TT), 0)
    second = lax.broadcasted_iota(jnp.int32, (TT, TT), 1)
    ahead = (first < second).astype(F32).astype(BF16)
    before = jnp.dot((hits[0] + hits[1]).astype(BF16), ahead, preferred_element_type=F32)
    return [jnp.sum(hit * before, axis=0, keepdims=True).astype(jnp.int32) for hit in hits]


def pack(ids_ref, x_ref, g_ref, s_ref):
    ids = ids_ref[...]
    slots = slots_of(ids)
    row = lax.broadcasted_iota(jnp.int32, (8 * CAP, TT), 0)
    hit = jnp.zeros((8 * CAP, TT), F32)
    for k in range(2):
        hit = hit + (ids[k:k + 1, :] * CAP + slots[k] == row).astype(F32)
    hot = hit.astype(BF16)
    for a, ref in enumerate((x_ref, g_ref)):
        rows = jnp.dot(hot, ref[...], preferred_element_type=F32).astype(BF16)
        for n in range(8):
            s_ref[n, a] = rows[n * CAP:(n + 1) * CAP, :]


class Arrival:
    def __init__(self, cp, arr, s, r, near):
        self.cp, self.arr, self.s, self.r, self.near = cp, arr, s, r, near
        q, e = places()
        self.q, self.e, self.h = q, e, lax.rem(e, 2)
        y, c = q // 2, lax.rem(q, 2)
        self.qu, self.qd, self.q2 = seq_at(y + 1, c), seq_at(y - 1, c), seq_at(y + 2, c)
        self.up, self.down, self.core = (self.qu, e), (self.qd, e), (y * 2 + 1 - c, e)
        self.pair = (q, e + 1 - 2 * self.h)
        self.across, self.cores = [], []

    def exchange(self):
        s, r, q, e, arr = self.s, self.r, self.q, self.e, self.arr
        x, z = e // 4, lax.rem(e, 4)

        def at(dx, dz):
            return lax.rem(x + dx, 4) * 4 + lax.rem(z + dz, 4)

        self.own = pltpu.make_async_copy(s.at[e // 2, arr], r.at[q, arr, x, z], self.near)
        self.own.start()
        self.parts = [
            self.cp.start(s.at[at(dx, dz) // 2, arr], r.at[q, arr, x, z], (q, at(dx, dz)))
            for dx in (2, 1, 3, 0) for dz in (2, 1, 3, 0) if (dx, dz) != (0, 0)]
    def move(self, shard, at, size, peer):
        ref = self.r.at[shard, self.arr, pl.ds(at, size)]
        return self.cp.start(ref, ref, peer)

    def pass_on(self, shard, at, size):
        self.cores.append(self.move(shard, at, size, self.core))

    def start(self):
        self.own.wait()
        for part in self.parts:
            part.wait_recv()
        h, q = self.h, self.q
        self.a = self.move(q, 2 * h, 1, self.up)
        self.b = self.move(q, 2 * h + 1, 1, self.down)
        self.a2 = self.move(q, 2 * h + 1, 1, self.up)
        self.b2 = self.move(q, 2 * h, 1, self.down)
        self.pass_on(q, 0, 4)

    def cross(self, shard, at, partner_at):
        self.across.append((shard, partner_at, self.move(shard, at, 1, self.pair)))

    def relay(self):
        h = self.h
        self.a.wait_recv()
        self.f = self.move(self.qd, 2 * h, 1, self.up)
        self.a3 = self.move(self.q, 2 - h, 1, self.up)
        self.pass_on(self.qd, 2 * h, 1)
        self.b.wait_recv()
        self.g = self.move(self.qu, 2 * h + 1, 1, self.down)
        self.b3 = self.move(self.q, 2 - h, 1, self.down)
        self.pass_on(self.qu, 2 * h + 1, 1)

    def middle(self):
        h = self.h
        self.a2.wait_recv()
        self.cross(self.qd, 3 * h, 3 - 3 * h)
        self.pass_on(self.qd, 2 * h + 1, 1)
        self.b2.wait_recv()
        self.cross(self.qu, 3 * h, 3 - 3 * h)
        self.pass_on(self.qu, 2 * h, 1)

    def late(self):
        h, q2 = self.h, self.q2
        self.f.wait_recv()
        self.cross(q2, 2 * h, 2 - 2 * h)
        self.pass_on(q2, 2 * h, 1)
        self.g.wait_recv()
        self.cross(q2, 2 * h + 1, 3 - 2 * h)
        self.pass_on(q2, 2 * h + 1, 1)

    def rest(self):
        self.a3.wait_recv()
        self.pass_on(self.qd, 2 - self.h, 1)
        self.b3.wait_recv()
        self.pass_on(self.qu, 2 - self.h, 1)
        for shard, at, copy in self.across:
            copy.wait_recv()
            self.pass_on(shard, at, 1)

    def end(self):
        for copy in self.cores:
            copy.wait_recv()


def resid_of(ids_ref, w_ref, t_ref, tp_ref, g_ref, probs_ref):
    ids = ids_ref[...]
    slots = slots_of(ids)
    weights = w_ref[...]
    table = jnp.concatenate(
        [ids[k:k + 1, :].astype(F32) for k in range(2)] + [slots[k].astype(F32) for k in range(2)]
        + [weights[k:k + 1, :] for k in range(2)] + [jnp.zeros((2, TT), F32)], axis=0).T
    lane = lax.broadcasted_iota(jnp.int32, (TT, 8 * CAP), 1)
    near = lax.broadcasted_iota(jnp.int32, (TT, 128), 1)
    total = g_ref[...].astype(F32)
    even = jnp.concatenate([t_ref[2 * n] for n in range(8)], axis=0)
    odd = jnp.concatenate([t_ref[2 * n + 1] for n in range(8)], axis=0)
    probs = []
    for k in range(2):
        name = table[:, k:k + 1].astype(jnp.int32)
        slot = table[:, 2 + k:3 + k].astype(jnp.int32)
        hot = (name * CAP + slot == lane).astype(F32).astype(BF16)
        route = jnp.dot(hot, even, preferred_element_type=F32) + jnp.dot(hot, odd, preferred_element_type=F32)
        total = total + table[:, 4 + k:5 + k] * route
        acc = jnp.zeros((TT, 128), F32)
        for n in range(8):
            row = tp_ref[2 * n, 0:1, :] + tp_ref[2 * n + 1, 0:1, :]
            acc = acc + jnp.where((name == n) & (slot == near), row, 0.0)
        probs.append(jnp.sum(acc, axis=1, keepdims=True))
    probs_ref[...] = jnp.concatenate(probs + [jnp.zeros((TT, 6), F32)], axis=1).T[:2, :]
    return total.astype(BF16)


def layer_kernel(ids_ref, w_ref, x_ref, g_ref, u, d, b_ref, c_ref, lr, st, sk, z_ref, wg_h, wu_h, wd_h, ow_h,
                 res_ref, probs_ref, gate_ref, input_ref, delta_ref, rates_ref, skipped_ref,
                 s_ref, r_ref, wg, wu, wd, gate, up, hid, dg, du, parts, pair, sums, land, final, probe, probes, mine,
                 t_ref, tp_ref, rate_ref, decay_ref, skip_ref, a, ear, bb, cb, dt, us, so,
                 ow, sent, lx, lz, kx, kz, jx, jz, inner, ys, s1s, dls,
                 term, terms, decays, part, other, both, three, send, recv, near):
    q, e = places()
    y, c = q // 2, lax.rem(q, 2)
    x, z = e // 4, lax.rem(e, 4)
    far = [(q, lax.rem(e + k, 16)) for k in range(1, 16)]
    rows = [(lax.rem(q + k, 8), e) for k in range(1, 8)]
    core = (y * 2 + 1 - c, e)
    xu, xd = (q, lax.rem(x + 1, 4) * 4 + z), (q, lax.rem(x + 3, 4) * 4 + z)
    zu, zd = (q, x * 4 + lax.rem(z + 1, 4)), (q, x * 4 + lax.rem(z + 3, 4))
    weights = [pltpu.make_async_copy(src.at[0], dst, near.at[n]) for n, (src, dst) in enumerate(
        ((wg_h, wg), (wu_h, wu), (wd_h, wd)))]
    late_load = pltpu.make_async_copy(ow_h, ow, near.at[5])
    terms[...] = jnp.zeros_like(terms)
    decays[...] = jnp.zeros_like(decays)
    knock(far + rows)
    pack(ids_ref, x_ref, g_ref, s_ref)
    for weight in weights:
        weight.start()
    late_load.start()
    greeted(far + rows)
    cp = Copies(send, recv)
    xs, gs = Arrival(cp, 0, s_ref, r_ref, near.at[3]), Arrival(cp, 1, s_ref, r_ref, near.at[4])
    xs.exchange()
    gs.exchange()
    scan = Forward(u, d, b_ref, c_ref, lr, st, sk, rate_ref, decay_ref, skip_ref, a, ear, bb, cb, dt, us, so)
    carry = scan.run(0, 40, scan.open())
    xs.start()
    carry = scan.run(40, 72, carry)
    xs.relay()
    gs.start()
    carry = scan.run(72, 80, carry)
    xs.middle()
    carry = scan.run(80, 96, carry)
    xs.late()
    scan.close(scan.run(96, TT, carry))
    xs.rest()
    gs.relay()
    xs.end()
    for weight in weights:
        weight.wait()

    def rows_of(arr, k):
        return jnp.concatenate([r_ref[:, arr, k, n].reshape(384, 256) for n in range(4)], axis=1)

    gate[...] = jnp.zeros_like(gate)
    up[...] = jnp.zeros_like(up)
    hid[...] = jnp.zeros_like(hid)

    def gate_and_up(first, last):
        @pl.loop(first, last)
        def _(k):
            deep = pl.ds(pl.multiple_of(k * 1024, 1024), 1024)
            lhs = rows_of(0, k)
            gate[...] += jnp.dot(lhs, wg[deep, :], preferred_element_type=F32)
            up[...] += jnp.dot(lhs, wu[deep, :], preferred_element_type=F32)

    gs.middle()
    gate_and_up(0, 2)
    gs.late()
    gate_and_up(2, 4)
    gs.rest()
    gs.end()

    @pl.loop(0, 4)
    def _(k):
        deep = pl.ds(pl.multiple_of(k * 1024, 1024), 1024)
        hid[...] += lax.dot_general(rows_of(1, k), wd[:, deep], NT, preferred_element_type=F32)

    v, w, h = gate[...], up[...], hid[...]
    sig = sigmoid(v)
    dg[...] = (h * w * sig * (1.0 + v * (1.0 - sig))).astype(BF16)
    gu = h * (v * sig)
    du[...] = gu.astype(BF16)
    order = [2, 1, 3, 0]
    four = [pl.multiple_of(lax.rem(x + n, 4) * 4, 4) for n in order]
    halves, rings, shares = [], [], []

    def multiply(i):
        deep = pl.ds(pl.multiple_of(four[i] * 256, 1024), 1024)
        part = lax.dot_general(dg[...], wg[deep, :], NT, preferred_element_type=F32)
        part = part + lax.dot_general(du[...], wu[deep, :], NT, preferred_element_type=F32)
        for n in range(4):
            parts[:, :, four[i] + n] = part[:, n * 256:(n + 1) * 256].reshape(4, 2, CAP, 256).astype(BF16)
        here = pl.ds(four[i], 4)
        halves.append(cp.start(parts.at[:, 1 - c, here], pair.at[:, here], core))

    def join(i):
        halves[i].wait_recv()

        @pl.loop(0, 16)
        def _(n):
            j, m = n // 4, four[i] + lax.rem(n, 4)
            sums[j, m] = added(BF16, parts[j, c, m], pair[j, m])

        ring = Ring(cp, y, (seq_at(y + 1, c), e), (seq_at(y - 1, c), e),
                    lambda d, half: (sums.at[d, pl.ds(four[i] + 2 * half, 2)],) * 2, land.at[i])
        ring.far()
        ring.near()
        rings.append(ring)

    two = add_rows(2)

    def leave(i):
        rings[i].last(two, (final.at[pl.ds(four[i], 2)], final.at[pl.ds(four[i] + 2, 2)]))
        for m in range(4):
            to = four[i] + lax.rem(z + m, 4)
            if order[i] == 0 and m == 0:
                own = pltpu.make_async_copy(final.at[to], t_ref.at[e], near.at[6])
                own.start()
                leave.own = own
            else:
                shares.append(cp.start(final.at[to], t_ref.at[e], (q, to)))

    multiply(0)
    held = gu * w
    held = held[:, :128] + held[:, 128:256] + held[:, 256:384] + held[:, 384:]
    probe[...] = jnp.broadcast_to(jnp.sum(held.T, axis=0, keepdims=True), (8, 384))
    tells = [cp.start(probe, probes.at[k], rows[k]) for k in range(7)]
    multiply(1)
    join(0)
    multiply(2)
    join(1)
    rings[0].second(two)
    multiply(3)
    join(2)
    rings[1].second(two)
    leave(0)
    join(3)
    rings[2].second(two)
    leave(1)
    for tell in tells:
        tell.wait_recv()
    total = probe[...]
    for k in range(7):
        total = total + probes[k]
    mine[...] = pltpu.roll(total, lax.rem(8 - q, 8) * CAP, 1)[:, :128]
    rings[3].second(two)
    own_probe = pltpu.make_async_copy(mine, tp_ref.at[e], near.at[7])
    own_probe.start()
    shares += [cp.start(mine, tp_ref.at[e], peer) for peer in far]
    leave(2)
    leave(3)
    own_probe.wait()
    leave.own.wait()
    for share in shares:
        share.wait_recv()

    def earlier_shards(src, land):
        copies = []
        for k in range(1, 8):
            copy = cp.make(src, land.at[k - 1], (lax.rem(q + 8 - k, 8), e))

            @pl.when(q >= k)
            def _(copy=copy):
                copy.start()
            copies.append(copy)

        def arrive():
            for k in range(1, 8):
                @pl.when(q + k < 8)
                def _(k=k):
                    copies[k - 1].wait_recv()

        def leave():
            for k in range(1, 8):
                @pl.when(q >= k)
                def _(k=k):
                    copies[k - 1].wait_send()
        return arrive, leave

    late_load.wait()
    res_ref[...] = resid_of(ids_ref, w_ref, t_ref, tp_ref, g_ref, probs_ref)
    resid = res_ref[...]

    def inner_part(d):
        for n in range(4):
            rows = pl.ds(pl.multiple_of(d * 2048, 2048) + 512 * n, 512)
            sent[d, n] = lax.dot_general(ow[rows, :], resid, NT, preferred_element_type=F32).astype(BF16)

    def x_block(i):
        def block(d, half):
            return (sent.at[d, pl.ds(2 * half, 2), pl.ds(128 * i, 128)],) * 2
        return block

    def z_block(i):
        def block(d, half):
            return (sent.at[pl.ds(2 * half, 2), d, pl.ds(256 + 128 * i, 128)],) * 2
        return block

    def then(ref):
        def block(d, half):
            return (ref.at[d, pl.ds(64 * half, 64)],) * 2
        return block

    def one(out, *refs):
        out[...] = added(out.dtype, *[ref[...] for ref in refs])

    rx = [Ring(cp, x, xu, xd, x_block(i), lx.at[i]) for i in range(2)]
    rz = [Ring(cp, z, zu, zd, z_block(i), lz.at[i]) for i in range(2)]
    sx = [Ring(cp, z, zu, zd, then(jx.at[i]), kx.at[i]) for i in range(2)]
    sz = [Ring(cp, x, xu, xd, then(jz.at[i]), kz.at[i]) for i in range(2)]
    inner_part(lax.rem(x + 2, 4))
    for ring in rx:
        ring.far()
    inner_part(lax.rem(x + 1, 4))
    inner_part(lax.rem(x + 3, 4))
    inner_part(x)
    for ring in rz:
        ring.far()
    for i in range(2):
        rx[i].near()
        rz[i].near()
    decays_in, decays_out = earlier_shards(decay_ref, decays)
    for i in range(2):
        rx[i].second(two)
        rz[i].second(two)
    for i in range(2):
        rx[i].last(two, (jx.at[i, pl.ds(0, 2)], jx.at[i, pl.ds(2, 2)]))
        sx[i].far()
        rz[i].last(two, (jz.at[i, pl.ds(0, 2)], jz.at[i, pl.ds(2, 2)]))
        sz[i].far()
        sx[i].near()
        sz[i].near()
    for i in range(2):
        sx[i].second(one)
        sz[i].second(one)
    def gradient(g):
        rows = pl.ds(g * 128, 128)
        act = z_ref[rows, :].astype(F32)
        spread(ys, g, (inner[rows, :] * act * sigmoid(act)).T)

    for i in range(2):
        sx[i].last(one, (inner.at[pl.ds(128 * i, 64)], inner.at[pl.ds(128 * i + 64, 64)]))
        gradient(i)
        sz[i].last(one, (inner.at[pl.ds(256 + 128 * i, 64)], inner.at[pl.ds(320 + 128 * i, 64)]))
        gradient(2 + i)

    zero = jnp.zeros((8, 128), F32)

    def summary(i, carry):
        t = TT - 1 - i
        grad = ys[at_token(t), :]
        return tuple(a[at_state(t, j), :] * (cb[at_state(t, j), :] * grad + carry[j]) for j in range(8))

    last = lax.fori_loop(0, TT, summary, (zero,) * 8, unroll=4)
    for j in range(8):
        term[octet(j), :] = last[j]
    terms_in, terms_out = earlier_shards(term, terms)

    for g in range(GR):
        rows = pl.ds(g * 128, 128)
        act = z_ref[rows, :].astype(F32)
        sig = sigmoid(act)
        gated = inner[rows, :] * so[pl.ds(g, TT, stride=8), :].T * sig * (1.0 + act * (1.0 - sig))
        gate_ref[rows, :] = gated.astype(BF16)

    decays_in()
    terms_in()
    rate = [rate_ref[octet(j), :] for j in range(8)]
    start = []
    for j in range(8):
        inc = zero
        for k in range(7, 0, -1):
            inc = terms[k - 1, octet(j), :] + decays[k - 1, octet(j), :] * inc
        start.append(inc)

    def step(i, carry):
        vs, sums, sk = carry
        t = TT - 1 - i
        here = at_token(t)
        grad = ys[here, :]
        size = dt[here, :]
        s1, dl = zero, zero
        nv, ns = [], []
        for j in range(8):
            spot = at_state(t, j)
            adj = cb[spot, :] * grad + vs[j]
            v = a[spot, :] * adj
            w = v * ear[spot, :]
            s1 = s1 + adj * bb[spot, :]
            dl = dl + rate[j] * w
            ns.append(sums[j] + size * w)
            nv.append(v)
        s1s[here, :] = s1 + pltpu.roll(s1, 4, 0)
        dls[here, :] = dl + pltpu.roll(dl, 4, 0)
        return tuple(nv), tuple(ns), sk + grad * us[here, :]

    vs, sums, sk = lax.fori_loop(0, TT, step, (tuple(start), (zero,) * 8, zero), unroll=4)
    for j in range(8):
        part[octet(j), :] = -rate[j] * sums[j]
    part[64:72, :] = sk
    swap = cp.start(part, other, (y * 2 + 1 - c, e))

    for g in range(GR):
        rows = pl.ds(g * 128, 128)
        mine = pl.ds(g, TT, stride=8)
        s1 = s1s[mine, :]
        inp = s1 * dt[mine, :] + skip_ref[g:g + 1, :] * ys[mine, :]
        input_ref[rows, :] = inp.T.astype(BF16)

    swap.wait_recv()
    both[...] = part[...] + other[...]
    shares = [cp.start(both, three.at[k - 1], (seq_at(y + k, c), e)) for k in range(1, 4)]

    for g in range(GR):
        rows = pl.ds(g * 128, 128)
        mine = pl.ds(g, TT, stride=8)
        step_grad = us[mine, :] * s1s[mine, :] - dls[mine, :]
        delta_ref[rows, :] = (step_grad.T * sigmoid(d[rows, :].astype(F32))).astype(BF16)

    for share in shares:
        share.wait_recv()
    both2 = both[...] + three[0] + three[1] + three[2]
    for j in range(8):
        for p in range(2):
            for g in range(GR):
                row = 8 * j + GR * p + g
                rates_ref[2 * j + p:2 * j + p + 1, g * 128:(g + 1) * 128] = both2[row:row + 1, :]
    for g in range(GR):
        skipped_ref[0:1, g * 128:(g + 1) * 128] = both2[64 + g:65 + g, :]
    decays_out()
    terms_out()
    cp.finish()


def finish_kernel(*refs):
    for src, dst in zip(refs[:7], refs[7:]):
        dst[...] = src[...]


def local(
    moe_input,
    out_grad,
    expert_ids,
    expert_route_weights,
    gate_weight,
    up_weight,
    down_weight,
    out_weight,
    scan_input,
    delta_raw,
    mixer_gate_branch,
    state_input,
    state_output,
    log_rates,
    skip_gain,
    block_states,
):
    block = pltpu.VMEM((4, 16, CAP, 256), BF16)
    results = pl.pallas_call(
        layer_kernel,
        out_shape=(shape((TT, 256), BF16), shape((2, TT))) + (shape((512, 128), BF16),) * 3
        + (shape((16, 512)), shape((1, 512))),
        in_specs=[VMEM] * 12 + [ANY] * 4,
        out_specs=(VMEM,) * 7,
        scratch_shapes=[
            pltpu.VMEM((8, 2, CAP, 256), BF16),
            pltpu.VMEM((8, 2, 4, 4, CAP, 256), BF16),
            pltpu.VMEM((4096, 512), BF16),
            pltpu.VMEM((4096, 512), BF16),
            pltpu.VMEM((512, 4096), BF16),
        ] + [pltpu.VMEM((384, 512), F32)] * 3 + [pltpu.VMEM((384, 512), BF16)] * 2
        + [pltpu.VMEM((4, 2, 16, CAP, 256), BF16), block, block, pltpu.VMEM((4, 8, 2, CAP, 256), BF16),
           pltpu.VMEM((16, CAP, 256), BF16), pltpu.VMEM((8, 384), F32), pltpu.VMEM((7, 8, 384), F32),
           pltpu.VMEM((8, 128), F32), pltpu.VMEM((16, CAP, 256), BF16), pltpu.VMEM((16, 8, 128), F32)]
        + [pltpu.VMEM((ROWS, 128), F32)] * 2 + [pltpu.VMEM((8, 128), F32)]
        + [pltpu.VMEM((TT * ROWS, 128), F32)] * 4 + [pltpu.VMEM((TT * 8, 128), F32)] * 3
        + [pltpu.VMEM((8192, 256), BF16), pltpu.VMEM((4, 4, 512, TT), BF16)]
        + [pltpu.VMEM((2, 8, 2, 128, TT), BF16)] * 2 + [pltpu.VMEM((2, 8, 64, TT), F32)] * 2
        + [pltpu.VMEM((2, 4, 128, TT), F32)] * 2 + [pltpu.VMEM((512, TT), F32)]
        + [pltpu.VMEM((TT * 8, 128), F32)] * 3
        + [pltpu.VMEM((ROWS, 128), F32)] + [pltpu.VMEM((7, ROWS, 128), F32)] * 2
        + [pltpu.VMEM((72, 128), F32)] * 3 + [pltpu.VMEM((3, 72, 128), F32)]
        + sems(211) + [pltpu.SemaphoreType.DMA((8,))],
        compiler_params=talk(1, 67043328),
        name="layer_backward",
    )(expert_ids.T, expert_route_weights.T, moe_input, out_grad, scan_input, delta_raw, state_input, state_output,
      log_rates, block_states, skip_gain.reshape(1, 512), mixer_gate_branch, gate_weight, up_weight, down_weight, out_weight)
    resid_grad, probs_grad, gate_grad, input_grad, delta_grad, rates_grad, skip_grad = pl.pallas_call(
        finish_kernel,
        out_shape=tuple(shape(r.shape, r.dtype) for r in results),
        in_specs=[VMEM] * 7,
        out_specs=(VMEM,) * 7,
        name="finish",
    )(*results)
    skip_grad = skip_grad.reshape(512)
    return (resid_grad, probs_grad.T, input_grad, delta_grad, gate_grad, rates_grad, skip_grad)


def solution(mesh):
    in_specs = (
        P("seq", "exp"),
        P("seq", "exp"),
        P("seq", None),
        P("seq", None),
        P("exp", None, "seq"),
        P("exp", None, "seq"),
        P("exp", "seq", None),
        P(None, "exp"),
        P("exp", "seq"),
        P("exp", "seq"),
        P("exp", "seq"),
        P(None, "seq"),
        P(None, "seq"),
        P(None, "exp"),
        P("exp"),
        P("seq", None, "exp"),
    )
    out_specs = (
        P("seq", "exp"),
        P("seq", None),
        P("exp", "seq"),
        P("exp", "seq"),
        P("exp", "seq"),
        P(None, "exp"),
        P("exp"),
    )
    return jax.shard_map(local, mesh=mesh, in_specs=in_specs, out_specs=out_specs, check_vma=False)
```
